32 devices in a mesh: tm: 8 (over z, x), pack: 4 (over y, core).
Axes of the slice: x: 2, y: 2, z: 4, core: 2. Of those that a mesh axis runs over, the one named last changes fastest.
Arguments:
- queries: bfloat16 [4, 4096, 1024], P('pack', 'tm'), may hold values from -8 to 8
- keys: bfloat16 [4, 4096, 1024], P('pack', 'tm'), may hold values from -8 to 8
- values: bfloat16 [4, 4096, 1024], P('pack', 'tm'), may hold values from -6 to 6
- w_out: bfloat16 [1024, 1024], replicated, may hold values from -0.1875 to 0.1875
- norm_gain: float32 [1024], replicated, may hold values from 0.1 to 1.9
- block_owner: int32 [4, 32, 1], P('pack', 'tm'), may hold values from 0 to 3; in each aligned block of 4 rows (0 to 3, 4 to 7, ..., all dimensions but the last counted through in order) at most 2 rows name the same one
- block_base: int32 [4, 32], P('pack', 'tm'), may hold values from 0 to 112
- frame_offset: int32 [4, 32, 128], P('pack', 'tm'), may hold values from 0 to 15, never falling along the last dimension, each value on 1 to 16 neighbouring positions
Outputs:
- encoded: bfloat16 [4, 4096, 1024], P('pack', 'tm')
- pooled: bfloat16 [4, 1024, 1024], P('pack', 'tm')
The draws below stay inside these ranges and needn't reach their ends.
Inputs may be any that keep to these rules, and one draw needn't show every extreme that they name: `block_owner`: among the 4 blocks of one device (aligned runs of the list), at most 2 name the same owner. `frame_offset`: within each block of 128 frames the offsets never fall and each of 0 to 15 occurs.
All inputs are finite; a program needn't handle non-finite values.
Results may differ from the reference program's by a relative error of at most 0.008.
Values may be sent and summed in bfloat16 or wider, within the bound.
No kernel may reach another device: no remote copies, remote signals or barrier semaphores. Data moves between devices by JAX's collectives and lax.ppermute only.
A program may use at most 128 MiB of HBM per device.

```python
import math
import jax
import jax.numpy as jnp
import numpy as np
from jax import lax

D = 1024
HEADS = 16
LANDMARKS = 256
TOK_DEV = 512
BLOCK = 128
WINDOW = 16
POOL_DEV = 128
GROUPS = 4
GROUP_FRAMES = 4096
ALL_LAND = 2048
DEV_BLOCKS = 4
GROUP_BLOCKS = 32
CAPACITY = 2
N_TM = 8


def drawn_field(key, own_salt):
    background = jnp.clip(jax.random.normal(jax.random.fold_in(key, own_salt), (GROUPS, N_TM, TOK_DEV, D), jnp.float32), -6.0, 6.0)
    aligned = background
    return aligned.reshape(GROUPS, GROUP_FRAMES, D)


def draw_queries(key, part):
    return drawn_field(key, 11).astype(jnp.bfloat16)


def draw_keys(key, part):
    return drawn_field(key, 12).astype(jnp.bfloat16)


def set_ends(values, key, least, largest):
    spot = [jax.random.randint(jax.random.fold_in(key, axis), (), 0, length) for axis, length in enumerate(values.shape)]
    widest = values.shape.index(max(values.shape))
    beside = spot[:widest] + [(spot[widest] + 1) % values.shape[widest]] + spot[widest + 1:]
    return values.at[tuple(spot)].set(least).at[tuple(beside)].set(largest)


def block_scale(rng, extent, cuts, smallest, largest):
    factor_of, own = 1.0, jax.random.fold_in(rng, 6)
    for dim, shards_of in cuts:
        draws = jnp.exp(jax.random.uniform(jax.random.fold_in(own, dim), (shards_of,), jnp.float32, smallest / len(cuts), largest / len(cuts)))
        factor_of = factor_of * jnp.repeat(draws, extent[dim] // shards_of).reshape([-1 if axis == dim else 1 for axis in range(len(extent))])
    return factor_of


def split_up(number_of, total, reach, skew):
    weights = [(1 << 20) // math.isqrt(standing ** skew) + 1 for standing in range(2, number_of + 1)]
    spare, given = total - reach - (number_of - 1), [1] * (number_of - 1)
    while spare > 0:
        candidates = [i for i in range(number_of - 1) if given[i] < reach]
        whole, budget = sum([weights[i] for i in candidates]), spare
        for i in candidates:
            addition = min(reach - given[i], max(1, budget * weights[i] // whole), spare)
            given[i] = given[i] + addition
            spare = spare - addition
    return np.array([reach] + given)


def ragged_sizes(rng, number_of, total, most, slope):
    if number_of == 2:
        one = jax.random.randint(rng, (), max(1, total - most), min(most, total - 1) + 1)
        return jnp.stack([one, total - one])
    tallies = jnp.asarray(split_up(number_of, total, most, slope), jnp.int32)
    twos = (number_of - 1) // 2
    giver, sink = tallies[1:1 + 2 * twos:2], tallies[2:2 + 2 * twos:2]
    slack = jnp.minimum(giver - 1, most - sink)
    passed = jax.random.randint(jax.random.fold_in(rng, 1), (twos,), 0, 1 << 20) % (slack + 1)
    tallies = tallies.at[1:1 + 2 * twos:2].set(giver - passed).at[2:2 + 2 * twos:2].set(sink + passed)
    return tallies[jax.random.permutation(jax.random.fold_in(rng, 2), number_of)]


def routed_block(stream_key, own, number, rows, amount, top, limit, slope):
    order = jax.random.permutation(stream_key, amount)
    packed, ordinary = portions_of(amount, rows * top, limit, slope, True), portions_of(amount, rows * top, limit, slope, False)
    places = jnp.arange(amount)

    def named(lengths, turn):
        used = int((lengths > 0).sum())
        fixed = max(1, used // 4)
        shifted = fixed + (places - fixed + turn * (used - fixed)) % max(1, amount - fixed)
        return jnp.zeros((amount,), jnp.int32).at[order[jnp.where(places < fixed, places, shifted)]].set(jnp.asarray(lengths, jnp.int32))

    lengths = jnp.where(number % 4 == 0, named(packed, number // 4), named(ordinary, number - number // 4 - 1))
    mixed = jax.random.permutation(jax.random.fold_in(own, 3), amount)
    giver, taker = mixed[0:amount // 2 * 2:2], mixed[1:amount // 2 * 2:2]
    margin = jnp.minimum(lengths[giver] - 1, limit - lengths[taker]) // 2
    margin = jnp.where((giver == order[0]) | (taker == order[0]) | (lengths[taker] == 0), 0, jnp.maximum(margin, 0))
    shifted = jax.random.randint(jax.random.fold_in(own, 4), (amount // 2,), 0, 1 << 20) % (margin + 1)
    lengths = lengths.at[giver].add(-shifted).at[taker].add(shifted)
    items = jnp.searchsorted(jnp.cumsum(lengths), jnp.arange(rows * top), side="right").astype(jnp.int32)
    grid = items.reshape(top, rows).T
    grid = grid[jax.random.permutation(jax.random.fold_in(own, 1), rows)]
    turn = jax.random.randint(jax.random.fold_in(own, 2), (rows, 1), 0, top)
    return jnp.take_along_axis(grid, (jnp.arange(top)[None, :] + turn) % top, axis=1)


def portions_of(number_of, total, limit, slope, full):
    weights = [(1 << 20) // math.isqrt(rank ** slope) + 1 for rank in range(1, number_of + 1)]
    largest = limit if full else min(limit, max(-(-total // number_of), total * weights[0] // sum(weights)))
    least = 1 if total - largest >= number_of - 1 else 0
    holding, rest = [largest] + [least] * (number_of - 1), total - largest - least * (number_of - 1)
    while rest > 0:
        free = [i for i in range(1, number_of) if holding[i] < largest] or [i for i in range(1, number_of) if holding[i] < limit]
        pool, budget = sum([weights[i] for i in free]), rest
        for i in free:
            extra = min(limit - holding[i], max(1, budget * weights[i] // pool), rest)
            holding[i] = holding[i] + extra
            rest = rest - extra
    return np.array(holding)


def scatter_about(own_key, shape, scale, limit, shards=(), held_as=jnp.bfloat16):
    gain = block_scale(own_key, shape, shards, -0.22, 0.18) if shards else 1.0
    drawn = jax.random.normal(own_key, shape, jnp.float32) * scale * gain
    return jnp.minimum(jnp.maximum(drawn, -limit), limit).astype(held_as)


def setup_inputs(seed: int = 0) -> dict:
    seeds = jax.random.split(jax.random.key(seed), 9)
    queries = draw_queries(jax.random.fold_in(seeds[8], 71), 0)
    keys = draw_keys(jax.random.fold_in(seeds[8], 71), 0)
    values = scatter_about(seeds[2], (GROUPS, GROUP_FRAMES, D), 1.0, 6.0, ((0, 4), (1, 8)))
    w_out = scatter_about(seeds[3], (D, D), D ** -0.5, 0.1875)
    norm_gain = jnp.clip(1.0 + 0.18 * jax.random.normal(seeds[4], (D,), jnp.float32), 0.1, 1.9)
    block_owner_keys = jax.random.split(jax.random.fold_in(seeds[5], 1), GROUPS * GROUP_BLOCKS // DEV_BLOCKS)
    block_owner_turns = jax.random.permutation(jax.random.fold_in(seeds[5], 3), GROUPS * GROUP_BLOCKS // DEV_BLOCKS)
    block_owner = jax.vmap(lambda own, number: routed_block(jax.random.fold_in(seeds[5], 2), own, number, DEV_BLOCKS, GROUPS, 1, CAPACITY, 2))(block_owner_keys, block_owner_turns).reshape((GROUPS, GROUP_BLOCKS, 1))
    block_base = set_ends(jax.random.randint(seeds[6], (GROUPS, GROUP_BLOCKS), 0, POOL_DEV - WINDOW + 1), jax.random.fold_in(seeds[6], 1), 0, POOL_DEV - WINDOW).astype(jnp.int32)
    frame_offset = jax.vmap(lambda own: jnp.searchsorted(jnp.cumsum(ragged_sizes(own, WINDOW, BLOCK, WINDOW, 1)), jnp.arange(BLOCK), side="right"))(jax.random.split(seeds[7], GROUPS * GROUP_BLOCKS)).reshape((GROUPS, GROUP_BLOCKS, BLOCK)).astype(jnp.int32)
    return {"queries": queries, "keys": keys, "values": values, "w_out": w_out, "norm_gain": norm_gain, "block_owner": block_owner, "block_base": block_base, "frame_offset": frame_offset}


def landmark_means(frames):
    span = TOK_DEV // LANDMARKS
    summed = frames.astype(jnp.float32).reshape(-1, span, D)
    return lax.optimization_barrier(jnp.mean(summed, axis=1)).astype(jnp.bfloat16)

def attend(query_rows, key_rows, value_rows):
    row_count = query_rows.shape[0]
    head_dim = D // HEADS
    query_heads = query_rows.astype(jnp.float32).reshape(row_count, HEADS, head_dim)
    key_heads = key_rows.astype(jnp.float32).reshape(-1, HEADS, head_dim)
    value_heads = value_rows.astype(jnp.float32).reshape(-1, HEADS, head_dim)
    scores = jnp.einsum('nhe,mhe->nhm', query_heads, key_heads) * head_dim ** (-0.5)
    weights = jnp.exp(scores - lax.optimization_barrier(jnp.max(scores, axis=-1, keepdims=True)))
    totals = lax.optimization_barrier(jnp.sum(weights, axis=-1))
    rounded = lax.optimization_barrier(weights.astype(jnp.bfloat16)).astype(jnp.float32)
    blended = jnp.einsum('nhm,mhe->nhe', rounded, value_heads) / totals[..., None]
    return blended.reshape(row_count, D).astype(jnp.bfloat16)

def reference(queries, keys, values, w_out, norm_gain, block_owner, block_base, frame_offset):
    row_block = math.gcd(GROUP_FRAMES, 512)
    encoded_groups = []
    for group_index in range(GROUPS):
        group_q = queries[group_index]
        group_k = keys[group_index]
        group_v = values[group_index]
        mark_q = landmark_means(group_q)
        mark_k = landmark_means(group_k)
        mark_v = lax.map(lambda pieces: attend(pieces[0], pieces[1], pieces[2]), (mark_q.reshape(N_TM, LANDMARKS, D), group_k.reshape(N_TM, TOK_DEV, D), group_v.reshape(N_TM, TOK_DEV, D))).reshape(ALL_LAND, D)
        attended = lax.map(lambda frame_block: attend(frame_block, mark_k, mark_v), group_q.reshape(-1, row_block, D)).reshape(GROUP_FRAMES, D)
        projected = jnp.dot(attended, w_out, preferred_element_type=jnp.float32)
        scaled = projected * lax.rsqrt(lax.optimization_barrier(jnp.mean(projected * projected, axis=-1, keepdims=True)) + 1e-06)
        encoded_groups.append((scaled * norm_gain).astype(jnp.bfloat16))
    encoded = jnp.stack(encoded_groups)
    positions = jnp.arange(GROUP_FRAMES, dtype=jnp.int32)
    shard_of = positions // TOK_DEV
    owner_of = jnp.repeat(block_owner[:, :, 0], BLOCK, axis=1)
    base_of = jnp.repeat(block_base, BLOCK, axis=1)
    target = (owner_of * N_TM + shard_of[None, :]) * POOL_DEV + base_of + frame_offset.reshape(GROUPS, GROUP_FRAMES)
    flat_target = target.reshape(-1).astype(jnp.int32)
    segment_total = GROUPS * N_TM * POOL_DEV
    pool_sums = jax.ops.segment_sum(encoded.reshape(-1, D).astype(jnp.float32), flat_target, num_segments=segment_total)
    counts = jax.ops.segment_sum(jnp.ones(flat_target.shape, jnp.float32), flat_target, num_segments=segment_total)
    pooled = (pool_sums / jnp.maximum(counts, 1.0)[:, None]).astype(jnp.bfloat16).reshape(GROUPS, N_TM * POOL_DEV, D)
    return (encoded, pooled)
```

```python
import functools
import math

import jax
import jax.numpy as jnp
from jax import lax
from jax.experimental import pallas as pl
from jax.experimental.pallas import tpu as pltpu
from jax.sharding import PartitionSpec as P

HEADS = 16
LANDMARKS = 256
BLOCK = 128
POOL_DEV = 128
WINDOW = 16
LANES = 128
ONES = 16
SLOTS = 2
META = 16
QUERY_BLOCK = 256
BF16 = jnp.bfloat16
F32 = jnp.float32


ANY = pl.BlockSpec(memory_space=pl.ANY)
VMEM = pl.BlockSpec(memory_space=pltpu.VMEM)
SMEM = pl.BlockSpec(memory_space=pltpu.SMEM)


def dot(a, b):
    return jnp.dot(a, b, preferred_element_type=F32)


def marks_kernel(team, streams, stream, head_dim, q_hbm, k_hbm, v_hbm, *refs):
    frames = q_hbm.shape[0]
    near, far = refs[:team], refs[team : 2 * team]
    packs, ins, in_sems, out_sems = refs[2 * team :]
    me = lax.axis_index("tm") % team
    span = frames // LANDMARKS
    strip_heads = LANES // head_dim
    scale = head_dim**-0.5 * math.log2(math.e)
    loads = []
    for d in range(team):
        column = pl.multiple_of((jnp.bitwise_xor(me, d) * streams + stream) * LANES, LANES)
        columns = pl.ds(column, LANES)
        three = [
            pltpu.make_async_copy(q_hbm.at[:, columns], packs.at[d, pl.ds(0, frames)], in_sems.at[d, 0]),
            pltpu.make_async_copy(k_hbm.at[:, columns], ins.at[d, 0], in_sems.at[d, 1]),
            pltpu.make_async_copy(v_hbm.at[:, columns], ins.at[d, 1], in_sems.at[d, 2]),
        ]
        for load in three:
            load.start()
        loads.append(three)
    row = lax.broadcasted_iota(jnp.int32, (LANDMARKS, frames), 0)
    frame = lax.broadcasted_iota(jnp.int32, (LANDMARKS, frames), 1)
    member = ((frame >= row * span) & (frame < (row + 1) * span)).astype(BF16)
    lane_row = lax.broadcasted_iota(jnp.int32, (LANES, LANDMARKS), 0)
    ones = jnp.ones((ONES, frames), BF16)
    stores = []
    for d in range(team):
        for load in loads[d]:
            load.wait()
        q, k, v = packs[d, pl.ds(0, frames)], ins[d, 0], ins[d, 1]
        mark_q = (dot(member, q) * (1.0 / span)).astype(BF16).astype(F32).T
        mark_k = (dot(member, k) * (1.0 / span)).astype(BF16)
        packs[d, pl.ds(frames, LANDMARKS)] = mark_k
        v_t = v.astype(F32).T.astype(BF16)
        heads = []
        for h in range(strip_heads):
            low = h * head_dim
            own = jnp.where((lane_row >= low) & (lane_row < low + head_dim), mark_q, 0.0).astype(BF16)
            scores = dot(k, own)
            top = jnp.max(scores, axis=0, keepdims=True)
            weights = jnp.exp2((scores - top) * scale).astype(BF16)
            mixed = dot(jnp.concatenate([v_t[low : low + head_dim], ones], axis=0), weights)
            heads.append(mixed[:head_dim] / mixed[head_dim : head_dim + 1])
        mark_v = jnp.concatenate(heads, axis=0).astype(BF16)
        for part in range(LANDMARKS // LANES):
            rows = pl.ds(frames + LANDMARKS + part * LANES, LANES)
            packs[d, rows] = mark_v[:, part * LANES : (part + 1) * LANES]
        two = [
            pltpu.make_async_copy(packs.at[d], near[d], out_sems.at[d, 0]),
            pltpu.make_async_copy(packs.at[d, pl.ds(frames, 2 * LANDMARKS)], far[d], out_sems.at[d, 1]),
        ]
        for store in two:
            store.start()
        stores += two
    for store in stores:
        store.wait()


def mark_strips(q, k, v, team, streams, stream, head_dim):
    frames = q.shape[0]
    near = jax.ShapeDtypeStruct((frames + 2 * LANDMARKS, LANES), BF16)
    far = jax.ShapeDtypeStruct((2 * LANDMARKS, LANES), BF16)
    out = pl.pallas_call(
        functools.partial(marks_kernel, team, streams, stream, head_dim),
        out_shape=[near] * team + [far] * team,
        in_specs=[ANY] * 3,
        out_specs=[ANY] * (2 * team),
        scratch_shapes=[
            pltpu.VMEM((team, frames + 2 * LANDMARKS, LANES), BF16),
            pltpu.VMEM((team, 2, frames, LANES), BF16),
            pltpu.SemaphoreType.DMA((team, 3)),
            pltpu.SemaphoreType.DMA((team, 2)),
        ],
        compiler_params=pltpu.CompilerParams(vmem_limit_bytes=24 << 20),
        name=f"marks_{stream}",
    )(q, k, v)
    return out[:team], out[team:]


def mix_kernel(team, sources, frames, head_dim, *refs):
    near, far = refs[:team], refs[team:sources]
    outs = refs[sources : sources + team]
    queries, mark_keys, mark_values, score_a, score_b, weight_a, weight_b, sems = refs[sources + team :]
    strip_heads = LANES // head_dim
    all_marks = sources * LANDMARKS
    scale = head_dim**-0.5 * math.log2(math.e)
    copies = []
    for s in range(sources):
        ref, base = (near[s], frames) if s < team else (far[s - team], 0)
        pairs = [(ref.at[pl.ds(base, LANDMARKS)], mark_keys.at[pl.ds(s * LANDMARKS, LANDMARKS)])]
        if s < team:
            pairs.append((ref.at[pl.ds(0, frames)], queries.at[s]))
        for part in range(LANDMARKS // LANES):
            for h in range(strip_heads):
                rows = pl.ds(base + LANDMARKS + part * LANES + h * head_dim, head_dim)
                columns = pl.ds(s * LANDMARKS + part * LANES, LANES)
                pairs.append((ref.at[rows], mark_values.at[h, pl.ds(0, head_dim), columns]))
        for source, target in pairs:
            copies.append(pltpu.make_async_copy(source, target, sems.at[len(copies)]))
            copies[-1].start()
    for h in range(strip_heads):
        mark_values[h, pl.ds(head_dim, ONES)] = jnp.ones((ONES, all_marks), BF16)
    for copy in copies:
        copy.wait()
    lane = lax.broadcasted_iota(jnp.int32, (QUERY_BLOCK, LANES), 1)
    chunk = LANDMARKS
    scores, weights = (score_a, score_b), (weight_a, weight_b)
    items = [(d, b, h) for d in range(team) for b in range(frames // QUERY_BLOCK) for h in range(strip_heads)]

    def own_queries(item):
        d, b, h = item
        rows = queries[d, pl.ds(b * QUERY_BLOCK, QUERY_BLOCK)].astype(F32)
        own = (lane >= h * head_dim) & (lane < (h + 1) * head_dim)
        return jnp.where(own, rows, 0.0).T.astype(BF16)

    def score(slot, c, query, top):
        rows = pl.ds(c * chunk, chunk)
        part = dot(mark_keys[rows], query)
        scores[slot][rows] = part
        most = jnp.max(part.reshape(chunk // 8, 8, QUERY_BLOCK), axis=0)
        return most if top is None else jnp.maximum(top, most)

    query, top, heads = own_queries(items[0]), None, []
    for c in range(sources):
        top = score(0, c, query, top)
    for i, (d, b, h) in enumerate(items):
        slot, more = i % 2, i + 1 < len(items)
        most, top = jnp.max(top, axis=0, keepdims=True), None
        if more:
            query = own_queries(items[i + 1])
        for c in range(sources):
            if more:
                top = score(1 - slot, c, query, top)
            rows = pl.ds(c * chunk, chunk)
            weights[slot][rows] = jnp.exp2((scores[slot][rows] - most) * scale).astype(BF16)
        mixed = dot(mark_values[h], weights[slot][...])
        heads.append(mixed[:head_dim] / mixed[head_dim : head_dim + 1])
        if h == strip_heads - 1:
            outs[d][pl.ds(b * QUERY_BLOCK, QUERY_BLOCK)] = jnp.concatenate(heads, axis=0).T.astype(BF16)
            heads = []


def mix_strips(near, far, frames, head_dim, stream):
    team, sources = len(near), len(near) + len(far)
    all_marks, strip_heads = sources * LANDMARKS, LANES // head_dim
    copies = sources * (1 + strip_heads * LANDMARKS // LANES) + team
    return pl.pallas_call(
        functools.partial(mix_kernel, team, sources, frames, head_dim),
        out_shape=[jax.ShapeDtypeStruct((frames, LANES), BF16)] * team,
        in_specs=[ANY] * sources,
        out_specs=[VMEM] * team,
        scratch_shapes=[
            pltpu.VMEM((team, frames, LANES), BF16),
            pltpu.VMEM((all_marks, LANES), BF16),
            pltpu.VMEM((strip_heads, head_dim + ONES, all_marks), BF16),
            pltpu.VMEM((all_marks, QUERY_BLOCK), F32),
            pltpu.VMEM((all_marks, QUERY_BLOCK), F32),
            pltpu.VMEM((all_marks, QUERY_BLOCK), BF16),
            pltpu.VMEM((all_marks, QUERY_BLOCK), BF16),
            pltpu.SemaphoreType.DMA((copies,)),
        ],
        compiler_params=pltpu.CompilerParams(vmem_limit_bytes=40 << 20),
        name=f"mix_{stream}",
    )(*near, *far)


def finish_kernel(team, streams, packs, blocks, owners, bases, offsets, w_out, gain, *refs):
    strips = refs[: team * streams]
    encoded = refs[team * streams]
    sends = refs[team * streams + 1 :]
    me = lax.axis_index("tm") % team
    my_pack = lax.axis_index("pack")
    width = streams * LANES
    model = w_out.shape[1]
    slots = packs * SLOTS * WINDOW
    owner = [owners[b, 0] for b in range(blocks)]
    starts = []
    for b in range(blocks):
        rank = jnp.int32(0)
        for a in range(b):
            rank = rank + jnp.where(owner[a] == owner[b], 1, 0)
        starts.append((jnp.bitwise_xor(owner[b], my_pack) * SLOTS + rank) * WINDOW)
    slot_row = lax.broadcasted_iota(jnp.int32, (slots, BLOCK), 0)
    slot_lane = lax.broadcasted_iota(jnp.int32, (1, slots), 1)
    hits, rows_to = [], jnp.zeros((1, slots), jnp.int32)
    for b in range(blocks):
        hits.append((slot_row == offsets[pl.ds(b, 1)] + starts[b]).astype(F32).astype(BF16))
        step = slot_lane - starts[b]
        rows_to = rows_to + jnp.where((step >= 0) & (step < WINDOW), step + (bases[0, b] + 1), 0)
    hit = jnp.concatenate(hits, axis=1)
    frame_counts = lax.dot_general(
        jnp.ones((META, blocks * BLOCK), BF16), hit, (((1,), (1,)), ((), ())), preferred_element_type=F32
    )
    for b in range(blocks):
        rows = pl.ds(b * BLOCK, BLOCK)
        projected = None
        for d in range(team):
            strip = jnp.concatenate([strips[s * team + d][rows] for s in range(streams)], axis=1)
            first = pl.multiple_of(jnp.bitwise_xor(me, d) * width, LANES)
            part = dot(strip, w_out[pl.ds(first, width)])
            projected = part if projected is None else projected + part
        power = jnp.mean(projected * projected, axis=-1, keepdims=True)
        encoded[rows] = (projected * lax.rsqrt(power + 1e-06) * gain[...]).astype(BF16)
    sums = dot(hit, encoded[...]).astype(BF16)
    meta_row = lax.broadcasted_iota(jnp.int32, (META, slots), 0)
    meta = jnp.where(meta_row == 0, rows_to.astype(F32), jnp.where(meta_row == 1, frame_counts, 0.0))
    part = SLOTS * WINDOW
    for e in range(packs):
        sends[e][pl.ds(0, part)] = sums[e * part : (e + 1) * part]
        sends[e][pl.ds(part, META)] = jnp.zeros((META, model), BF16)
        sends[e][pl.ds(part, META), pl.ds(0, slots)] = meta.astype(BF16)


def finish(strips, w_out, gain, owners, bases, offsets, team, streams, packs):
    frames, model = strips[0].shape[0], w_out.shape[1]
    blocks = owners.shape[0]
    send = jax.ShapeDtypeStruct((SLOTS * WINDOW + META, model), BF16)
    out = pl.pallas_call(
        functools.partial(finish_kernel, team, streams, packs, blocks),
        out_shape=[jax.ShapeDtypeStruct((frames, model), BF16)] + [send] * packs,
        in_specs=[SMEM, SMEM] + [VMEM] * (3 + len(strips)),
        out_specs=[VMEM] * (1 + packs),
        compiler_params=pltpu.CompilerParams(vmem_limit_bytes=24 << 20),
        name="finish",
    )(owners, bases, offsets, w_out, gain, *strips)
    return out[0], out[1:]


def pool_kernel(packs, *refs):
    got, pooled = refs[:packs], refs[packs]
    part = SLOTS * WINDOW
    slots = packs * part
    lane = lax.broadcasted_iota(jnp.int32, (1, slots), 1)
    rows_to, counts = jnp.zeros((1, slots), F32), jnp.zeros((1, slots), F32)
    for e in range(packs):
        meta = got[e][pl.ds(part, META), pl.ds(0, slots)].astype(F32)
        mine = (lane >= e * part) & (lane < (e + 1) * part)
        rows_to = jnp.where(mine, meta[0:1], rows_to)
        counts = jnp.where(mine, meta[1:2], counts)
    row = lax.broadcasted_iota(jnp.int32, (POOL_DEV, slots), 0)
    place = row + 1 == rows_to.astype(jnp.int32)
    total = jnp.sum(jnp.where(place, counts, 0.0), axis=1, keepdims=True)
    rows = jnp.concatenate([got[e][pl.ds(0, part)] for e in range(packs)], axis=0)
    sums = dot(place.astype(F32).astype(BF16), rows)
    pooled[...] = (sums / jnp.maximum(total, 1.0)).astype(BF16)


def pool(got):
    return pl.pallas_call(
        functools.partial(pool_kernel, len(got)),
        out_shape=jax.ShapeDtypeStruct((POOL_DEV, got[0].shape[1]), BF16),
        in_specs=[VMEM] * len(got),
        out_specs=VMEM,
        name="pool",
    )(*got)


def swap(array, axis, size, bits):
    return lax.ppermute(array, axis, [(i, i ^ bits) for i in range(size)])


def local(team, queries, keys, values, w_out, norm_gain, block_owner, block_base, frame_offset):
    q, k, v = queries[0], keys[0], values[0]
    frames, model = q.shape
    tm, packs = lax.axis_size("tm"), lax.axis_size("pack")
    head_dim = model // HEADS
    streams = model // team // LANES
    near, far = [], []
    for s in range(streams):
        near_out, far_out = mark_strips(q, k, v, team, streams, s, head_dim)
        far.append([swap(far_out[d], "tm", tm, other + d) for other in range(team, tm, team) for d in range(team)])
        near.append([near_out[0]] + [swap(near_out[d], "tm", tm, d) for d in range(1, team)])
    strips = []
    for s in range(streams):
        mixed = mix_strips(near[s], far[s], frames, head_dim, s)
        strips += [mixed[0]] + [swap(mixed[d], "tm", tm, d) for d in range(1, team)]
    encoded, sends = finish(
        strips, w_out, norm_gain[None], block_owner[0], block_base, frame_offset[0], team, streams, packs
    )
    got = [sends[0]] + [swap(sends[e], "pack", packs, e) for e in range(1, packs)]
    return encoded[None], pool(got)[None]


def solution(mesh):
    team = mesh.shape["tm"] // 2
    return jax.shard_map(
        functools.partial(local, team),
        mesh=mesh,
        in_specs=(
            P("pack", "tm", None),
            P("pack", "tm", None),
            P("pack", "tm", None),
            P(),
            P(),
            P("pack", "tm", None),
            P("pack", "tm"),
            P("pack", "tm", None),
        ),
        out_specs=(P("pack", "tm", None), P("pack", "tm", None)),
        check_vma=False,
    )
```

```python
import functools
import math

import jax
import jax.numpy as jnp
from jax import lax
from jax.experimental import pallas as pl
from jax.experimental.pallas import tpu as pltpu
from jax.sharding import PartitionSpec as P


HEADS = 16
LANDMARKS = 256
BLOCK = 128
POOL_DEV = 128
WINDOW = 16
LANES = 128
ONES = 16
SLOTS = 2
META = 16
QUERY_BLOCK = 256
BF16 = jnp.bfloat16
F32 = jnp.float32


ANY = pl.BlockSpec(memory_space=pl.ANY)
HBM = pl.BlockSpec(memory_space=pltpu.HBM)
VMEM = pl.BlockSpec(memory_space=pltpu.VMEM)
SMEM = pl.BlockSpec(memory_space=pltpu.SMEM)


def dot(a, b):
    return jnp.dot(a, b, preferred_element_type=F32)


def marks_kernel(team, streams, head_dim, q_hbm, k_hbm, v_hbm, *refs):
    frames = q_hbm.shape[0]
    strips = team * streams
    near, far = refs[:strips], refs[strips : 2 * strips]
    packs, ins, score_a, score_b, in_sems, out_sems = refs[2 * strips :]
    me = lax.axis_index("tm") % team
    span = frames // LANDMARKS
    strip_heads = LANES // head_dim
    scale = head_dim**-0.5 * math.log2(math.e)
    loads = []
    for i in range(strips):
        stream, d = divmod(i, team)
        column = pl.multiple_of((jnp.bitwise_xor(me, d) * streams + stream) * LANES, LANES)
        columns = pl.ds(column, LANES)
        three = [
            pltpu.make_async_copy(q_hbm.at[:, columns], packs.at[i, pl.ds(0, frames)], in_sems.at[i, 0]),
            pltpu.make_async_copy(k_hbm.at[:, columns], ins.at[i, 0], in_sems.at[i, 1]),
            pltpu.make_async_copy(v_hbm.at[:, columns], ins.at[i, 1], in_sems.at[i, 2]),
        ]
        for load in three:
            load.start()
        loads.append(three)
    row = lax.broadcasted_iota(jnp.int32, (LANDMARKS, frames), 0)
    frame = lax.broadcasted_iota(jnp.int32, (LANDMARKS, frames), 1)
    member = ((frame >= row * span) & (frame < (row + 1) * span)).astype(BF16)
    lane_row = lax.broadcasted_iota(jnp.int32, (LANES, LANDMARKS), 0)
    ones = jnp.ones((ONES, frames), BF16)
    scores = (score_a, score_b)
    stores = []

    def prepare(i):
        for load in loads[i]:
            load.wait()
        mark_q = (dot(member, packs[i, pl.ds(0, frames)]) * (1.0 / span)).astype(BF16).astype(F32).T
        mark_k = (dot(member, ins[i, 0]) * (1.0 / span)).astype(BF16)
        packs[i, pl.ds(frames, LANDMARKS)] = mark_k
        return mark_q, ins[i, 1].astype(F32).T.astype(BF16)

    def score(i, h, slot, mark_q):
        low = h * head_dim
        own = jnp.where((lane_row >= low) & (lane_row < low + head_dim), mark_q, 0.0).astype(BF16)
        part = dot(ins[i, 0], own)
        scores[slot][...] = part
        return jnp.max(part, axis=0, keepdims=True)

    items = [(i, h) for i in range(strips) for h in range(strip_heads)]
    mark_q, v_next = prepare(0)
    top, heads = score(0, 0, 0, mark_q), []
    for n, (i, h) in enumerate(items):
        slot, most, v_t = n % 2, top, v_next
        if n + 1 < len(items):
            j, g = items[n + 1]
            if g == 0:
                mark_q, v_next = prepare(j)
            top = score(j, g, 1 - slot, mark_q)
        weights = jnp.exp2((scores[slot][...] - most) * scale).astype(BF16)
        mixed = dot(jnp.concatenate([v_t[h * head_dim : (h + 1) * head_dim], ones], axis=0), weights)
        heads.append(mixed[:head_dim] / mixed[head_dim : head_dim + 1])
        if h < strip_heads - 1:
            continue
        mark_v, heads = jnp.concatenate(heads, axis=0).astype(BF16), []
        for part in range(LANDMARKS // LANES):
            rows = pl.ds(frames + LANDMARKS + part * LANES, LANES)
            packs[i, rows] = mark_v[:, part * LANES : (part + 1) * LANES]
        two = [
            pltpu.make_async_copy(packs.at[i], near[i], out_sems.at[i, 0]),
            pltpu.make_async_copy(packs.at[i, pl.ds(frames, 2 * LANDMARKS)], far[i], out_sems.at[i, 1]),
        ]
        for store in two:
            store.start()
        stores += two
    for store in stores:
        store.wait()


def mark_strips(q, k, v, team, streams, head_dim):
    frames = q.shape[0]
    strips = team * streams
    near = jax.ShapeDtypeStruct((frames + 2 * LANDMARKS, LANES), BF16)
    far = jax.ShapeDtypeStruct((2 * LANDMARKS, LANES), BF16)
    out = pl.pallas_call(
        functools.partial(marks_kernel, team, streams, head_dim),
        out_shape=[near] * strips + [far] * strips,
        in_specs=[HBM] * 3,
        out_specs=[ANY] * (2 * strips),
        scratch_shapes=[
            pltpu.VMEM((strips, frames + 2 * LANDMARKS, LANES), BF16),
            pltpu.VMEM((strips, 2, frames, LANES), BF16),
            pltpu.VMEM((frames, LANDMARKS), F32),
            pltpu.VMEM((frames, LANDMARKS), F32),
            pltpu.SemaphoreType.DMA((strips, 3)),
            pltpu.SemaphoreType.DMA((strips, 2)),
        ],
        compiler_params=pltpu.CompilerParams(vmem_limit_bytes=60 << 20),
        name="marks",
    )(q, k, v)
    return out[:strips], out[strips:]


def mix_kernel(team, sources, frames, head_dim, *refs):
    near, far = refs[:team], refs[team:sources]
    outs = refs[sources : sources + team]
    queries, mark_keys, mark_values, mixed_all, weight_a, weight_b, scores, sems = refs[sources + team :]
    strip_heads = LANES // head_dim
    all_marks = sources * LANDMARKS
    scale = head_dim**-0.5 * math.log2(math.e)
    copies = []
    for s in range(sources):
        ref, base = (near[s], frames) if s < team else (far[s - team], 0)
        pairs = [(ref.at[pl.ds(base, LANDMARKS)], mark_keys.at[pl.ds(s * LANDMARKS, LANDMARKS)])]
        if s < team:
            pairs.append((ref.at[pl.ds(0, frames)], queries.at[s]))
        for part in range(LANDMARKS // LANES):
            for h in range(strip_heads):
                rows = pl.ds(base + LANDMARKS + part * LANES + h * head_dim, head_dim)
                columns = pl.ds(s * LANDMARKS + part * LANES, LANES)
                pairs.append((ref.at[rows], mark_values.at[h, pl.ds(0, head_dim), columns]))
        for source, target in pairs:
            copies.append(pltpu.make_async_copy(source, target, sems.at[len(copies)]))
            copies[-1].start()
    for h in range(strip_heads):
        mark_values[h, pl.ds(head_dim, ONES)] = jnp.ones((ONES, all_marks), BF16)
    for copy in copies:
        copy.wait()
    lane = lax.broadcasted_iota(jnp.int32, (QUERY_BLOCK, LANES), 1)
    chunk = math.gcd(all_marks, 512)
    chunks = all_marks // chunk
    blocks = frames // QUERY_BLOCK
    weights = (weight_a, weight_b)
    items = [(d, b, h) for d in range(team) for b in range(blocks) for h in range(strip_heads)]

    def own_queries(rows, h):
        own = (lane >= h * head_dim) & (lane < (h + 1) * head_dim)
        return jnp.where(own, rows.astype(F32), 0.0).T.astype(BF16)

    least, most = jnp.full((1, QUERY_BLOCK), 1.0, F32), jnp.full((1, QUERY_BLOCK), 1.0, F32)
    heads = []
    for i in range(len(items) + 1):
        if i < len(items):
            d, b, h = items[i]
            query = own_queries(queries[d, pl.ds(b * QUERY_BLOCK, QUERY_BLOCK)], h)
        for c in range(chunks):
            rows = pl.ds(c * chunk, chunk)
            if i < len(items):
                weights[i % 2][rows] = jnp.exp2(dot(mark_keys[rows], query) * scale).astype(BF16)
            if i > 0:
                part = dot(mark_values[items[i - 1][2], :, rows], weights[1 - i % 2][rows])
                mixed = part if c == 0 else mixed + part
        if i == 0:
            continue
        d, b, h = items[i - 1]
        total = mixed[head_dim : head_dim + 1]
        least, most = jnp.minimum(least, total), jnp.maximum(most, total)
        heads.append(mixed[:head_dim] / total)
        if h == strip_heads - 1:
            mixed_all[d, pl.ds(b * QUERY_BLOCK, QUERY_BLOCK)] = jnp.concatenate(heads, axis=0).T.astype(BF16)
            heads = []
    unsafe = jnp.sum(jnp.where((least > 2.0**-40) & (most < 2.0**100), 0, 1))

    @pl.when(unsafe > 0)
    def _():
        def exact(i, carry):
            d, b = i // blocks, i % blocks
            block = pl.ds(pl.multiple_of(b * QUERY_BLOCK, QUERY_BLOCK), QUERY_BLOCK)
            parts = []
            for h in range(strip_heads):
                query = own_queries(queries[d, block], h)

                def score(c, top):
                    rows = pl.ds(pl.multiple_of(c * chunk, chunk), chunk)
                    part = dot(mark_keys[rows], query)
                    scores[rows] = part
                    return jnp.maximum(top, jnp.max(part, axis=0, keepdims=True))

                top = lax.fori_loop(0, chunks, score, jnp.full((1, QUERY_BLOCK), -jnp.inf, F32))

                def weigh(c, total):
                    rows = pl.ds(pl.multiple_of(c * chunk, chunk), chunk)
                    weight_a[rows] = jnp.exp2((scores[rows] - top) * scale).astype(BF16)
                    return total

                lax.fori_loop(0, chunks, weigh, 0)
                mixed = dot(mark_values[h], weight_a[...])
                parts.append(mixed[:head_dim] / mixed[head_dim : head_dim + 1])
            mixed_all[d, block] = jnp.concatenate(parts, axis=0).T.astype(BF16)
            return carry

        lax.fori_loop(0, team * blocks, exact, 0)

    for d in range(team):
        outs[d][...] = mixed_all[d]


def mix_strips(near, far, frames, head_dim):
    team, sources = len(near), len(near) + len(far)
    all_marks, strip_heads = sources * LANDMARKS, LANES // head_dim
    copies = sources * (1 + strip_heads * LANDMARKS // LANES) + team
    return pl.pallas_call(
        functools.partial(mix_kernel, team, sources, frames, head_dim),
        out_shape=[jax.ShapeDtypeStruct((frames, LANES), BF16)] * team,
        in_specs=[ANY] * sources,
        out_specs=[VMEM] * team,
        scratch_shapes=[
            pltpu.VMEM((team, frames, LANES), BF16),
            pltpu.VMEM((all_marks, LANES), BF16),
            pltpu.VMEM((strip_heads, head_dim + ONES, all_marks), BF16),
            pltpu.VMEM((team, frames, LANES), BF16),
            pltpu.VMEM((all_marks, QUERY_BLOCK), BF16),
            pltpu.VMEM((all_marks, QUERY_BLOCK), BF16),
            pltpu.VMEM((all_marks, QUERY_BLOCK), F32),
            pltpu.SemaphoreType.DMA((copies,)),
        ],
        compiler_params=pltpu.CompilerParams(vmem_limit_bytes=32 << 20),
    )(*near, *far)


def finish_kernel(team, streams, packs, blocks, owners, bases, offsets, w_out, gain, *refs):
    strips = refs[: team * streams]
    encoded = refs[team * streams]
    sends = refs[team * streams + 1 :]
    me = lax.axis_index("tm") % team
    my_pack = lax.axis_index("pack")
    width = streams * LANES
    model = w_out.shape[1]
    slots = packs * SLOTS * WINDOW
    owner = [owners[b, 0] for b in range(blocks)]
    starts = []
    for b in range(blocks):
        rank = jnp.int32(0)
        for a in range(b):
            rank = rank + jnp.where(owner[a] == owner[b], 1, 0)
        starts.append((jnp.bitwise_xor(owner[b], my_pack) * SLOTS + rank) * WINDOW)
    slot_row = lax.broadcasted_iota(jnp.int32, (slots, BLOCK), 0)
    slot_lane = lax.broadcasted_iota(jnp.int32, (1, slots), 1)
    hits, rows_to = [], jnp.zeros((1, slots), jnp.int32)
    for b in range(blocks):
        hits.append((slot_row == offsets[pl.ds(b, 1)] + starts[b]).astype(F32).astype(BF16))
        step = slot_lane - starts[b]
        rows_to = rows_to + jnp.where((step >= 0) & (step < WINDOW), step + (bases[0, b] + 1), 0)
    hit = jnp.concatenate(hits, axis=1)
    frame_counts = lax.dot_general(
        jnp.ones((META, blocks * BLOCK), BF16), hit, (((1,), (1,)), ((), ())), preferred_element_type=F32
    )
    for b in range(blocks):
        rows = pl.ds(b * BLOCK, BLOCK)
        projected = None
        for d in range(team):
            strip = jnp.concatenate([strips[s * team + d][rows] for s in range(streams)], axis=1)
            first = pl.multiple_of(jnp.bitwise_xor(me, d) * width, LANES)
            part = dot(strip, w_out[pl.ds(first, width)])
            projected = part if projected is None else projected + part
        power = jnp.mean(projected * projected, axis=-1, keepdims=True)
        encoded[rows] = (projected * lax.rsqrt(power + 1e-06) * gain[...]).astype(BF16)
    sums = dot(hit, encoded[...]).astype(BF16)
    meta_row = lax.broadcasted_iota(jnp.int32, (META, slots), 0)
    meta = jnp.where(meta_row == 0, rows_to.astype(F32), jnp.where(meta_row == 1, frame_counts, 0.0))
    part = SLOTS * WINDOW
    for e in range(packs):
        sends[e][pl.ds(0, part)] = sums[e * part : (e + 1) * part]
        sends[e][pl.ds(part, META)] = jnp.zeros((META, model), BF16)
        sends[e][pl.ds(part, META), pl.ds(0, slots)] = meta.astype(BF16)


def finish(strips, w_out, gain, owners, bases, offsets, team, streams, packs):
    frames, model = strips[0].shape[0], w_out.shape[1]
    blocks = owners.shape[0]
    send = jax.ShapeDtypeStruct((SLOTS * WINDOW + META, model), BF16)
    out = pl.pallas_call(
        functools.partial(finish_kernel, team, streams, packs, blocks),
        out_shape=[jax.ShapeDtypeStruct((frames, model), BF16)] + [send] * packs,
        in_specs=[SMEM, SMEM] + [VMEM] * (3 + len(strips)),
        out_specs=[VMEM] * (1 + packs),
        compiler_params=pltpu.CompilerParams(vmem_limit_bytes=24 << 20),
        name="finish",
    )(owners, bases, offsets, w_out, gain, *strips)
    return out[0], out[1:]


def pool_kernel(packs, *refs):
    got, pooled = refs[:packs], refs[packs]
    part = SLOTS * WINDOW
    slots = packs * part
    lane = lax.broadcasted_iota(jnp.int32, (1, slots), 1)
    rows_to, counts = jnp.zeros((1, slots), F32), jnp.zeros((1, slots), F32)
    for e in range(packs):
        meta = got[e][pl.ds(part, META), pl.ds(0, slots)].astype(F32)
        mine = (lane >= e * part) & (lane < (e + 1) * part)
        rows_to = jnp.where(mine, meta[0:1], rows_to)
        counts = jnp.where(mine, meta[1:2], counts)
    row = lax.broadcasted_iota(jnp.int32, (POOL_DEV, slots), 0)
    place = row + 1 == rows_to.astype(jnp.int32)
    total = jnp.sum(jnp.where(place, counts, 0.0), axis=1, keepdims=True)
    rows = jnp.concatenate([got[e][pl.ds(0, part)] for e in range(packs)], axis=0)
    sums = dot(place.astype(F32).astype(BF16), rows)
    pooled[...] = (sums / jnp.maximum(total, 1.0)).astype(BF16)


def pool(got):
    return pl.pallas_call(
        functools.partial(pool_kernel, len(got)),
        out_shape=jax.ShapeDtypeStruct((POOL_DEV, got[0].shape[1]), BF16),
        in_specs=[VMEM] * len(got),
        out_specs=VMEM,
        compiler_params=pltpu.CompilerParams(vmem_limit_bytes=8 << 20),
        name="pool",
    )(*got)


def swap(array, axis, size, bits):
    return lax.ppermute(array, axis, [(i, i ^ bits) for i in range(size)])


def local(team, queries, keys, values, w_out, norm_gain, block_owner, block_base, frame_offset):
    q, k, v = queries[0], keys[0], values[0]
    frames, model = q.shape
    tm, packs = lax.axis_size("tm"), lax.axis_size("pack")
    head_dim = model // HEADS
    streams = model // team // LANES
    near_out, far_out = mark_strips(q, k, v, team, streams, head_dim)
    strips = []
    for s in range(streams):
        mine = range(s * team, (s + 1) * team)
        far = [
            swap(far_out[i], "tm", tm, other + d)
            for other in range(team, tm, team)
            for d, i in enumerate(mine)
        ]
        near = [near_out[s * team]]
        near += [swap(near_out[mine[d]], "tm", tm, d) for d in range(1, team)]
        mixed = mix_strips(near, far, frames, head_dim)
        strips += [mixed[0]] + [swap(mixed[d], "tm", tm, d) for d in range(1, team)]
    encoded, sends = finish(
        strips, w_out, norm_gain[None], block_owner[0], block_base, frame_offset[0], team, streams, packs
    )
    got = [sends[0]] + [swap(sends[e], "pack", packs, e) for e in range(1, packs)]
    return encoded[None], pool(got)[None]


def solution(mesh):
    tm = mesh.shape["tm"]
    team = tm // 2
    return jax.shard_map(
        functools.partial(local, team),
        mesh=mesh,
        in_specs=(
            P("pack", "tm", None),
            P("pack", "tm", None),
            P("pack", "tm", None),
            P(),
            P(),
            P("pack", "tm", None),
            P("pack", "tm"),
            P("pack", "tm", None),
        ),
        out_specs=(P("pack", "tm", None), P("pack", "tm", None)),
        check_vma=False,
    )
```

```python
import functools
import math

import jax
import jax.numpy as jnp
from jax import lax
from jax.experimental import pallas as pl
from jax.experimental.pallas import tpu as pltpu
from jax.sharding import PartitionSpec as P


HEADS = 16
LANDMARKS = 256
BLOCK = 128
POOL_DEV = 128
WINDOW = 16
LANES = 128
ONES = 16
SLOTS = 2
META = 16
QUERY_BLOCK = 256
BF16 = jnp.bfloat16
F32 = jnp.float32


ANY = pl.BlockSpec(memory_space=pl.ANY)
HBM = pl.BlockSpec(memory_space=pltpu.HBM)
VMEM = pl.BlockSpec(memory_space=pltpu.VMEM)
SMEM = pl.BlockSpec(memory_space=pltpu.SMEM)


def dot(a, b):
    return jnp.dot(a, b, preferred_element_type=F32)


def marks_kernel(team, streams, stream, head_dim, q_hbm, k_hbm, v_hbm, *refs):
    frames = q_hbm.shape[0]
    strips = team
    near, far = refs[:strips], refs[strips : 2 * strips]
    packs, ins, score_a, score_b, in_sems, out_sems = refs[2 * strips :]
    me = lax.axis_index("tm") % team
    span = frames // LANDMARKS
    strip_heads = LANES // head_dim
    scale = head_dim**-0.5 * math.log2(math.e)
    loads = []
    for i in range(strips):
        column = pl.multiple_of((jnp.bitwise_xor(me, i) * streams + stream) * LANES, LANES)
        columns = pl.ds(column, LANES)
        three = [
            pltpu.make_async_copy(q_hbm.at[:, columns], packs.at[i, pl.ds(0, frames)], in_sems.at[i, 0]),
            pltpu.make_async_copy(k_hbm.at[:, columns], ins.at[i, 0], in_sems.at[i, 1]),
            pltpu.make_async_copy(v_hbm.at[:, columns], ins.at[i, 1], in_sems.at[i, 2]),
        ]
        for load in three:
            load.start()
        loads.append(three)
    row = lax.broadcasted_iota(jnp.int32, (LANDMARKS, frames), 0)
    frame = lax.broadcasted_iota(jnp.int32, (LANDMARKS, frames), 1)
    member = ((frame >= row * span) & (frame < (row + 1) * span)).astype(BF16)
    lane_row = lax.broadcasted_iota(jnp.int32, (LANES, LANDMARKS), 0)
    ones = jnp.ones((ONES, frames), BF16)
    scores = (score_a, score_b)
    stores = []

    def prepare(i):
        for load in loads[i]:
            load.wait()
        mark_q = (dot(member, packs[i, pl.ds(0, frames)]) * (1.0 / span)).astype(BF16).astype(F32).T
        mark_k = (dot(member, ins[i, 0]) * (1.0 / span)).astype(BF16)
        packs[i, pl.ds(frames, LANDMARKS)] = mark_k
        return mark_q, ins[i, 1].astype(F32).T.astype(BF16)

    def score(i, h, slot, mark_q):
        low = h * head_dim
        own = jnp.where((lane_row >= low) & (lane_row < low + head_dim), mark_q, 0.0).astype(BF16)
        part = dot(ins[i, 0], own)
        scores[slot][...] = part
        return jnp.max(part, axis=0, keepdims=True)

    items = [(i, h) for i in range(strips) for h in range(strip_heads)]
    mark_q, v_next = prepare(0)
    top, heads = score(0, 0, 0, mark_q), []
    for n, (i, h) in enumerate(items):
        slot, most, v_t = n % 2, top, v_next
        if n + 1 < len(items):
            j, g = items[n + 1]
            if g == 0:
                mark_q, v_next = prepare(j)
            top = score(j, g, 1 - slot, mark_q)
        weights = jnp.exp2((scores[slot][...] - most) * scale).astype(BF16)
        mixed = dot(jnp.concatenate([v_t[h * head_dim : (h + 1) * head_dim], ones], axis=0), weights)
        heads.append(mixed[:head_dim] / mixed[head_dim : head_dim + 1])
        if h < strip_heads - 1:
            continue
        mark_v, heads = jnp.concatenate(heads, axis=0).astype(BF16), []
        for part in range(LANDMARKS // LANES):
            rows = pl.ds(frames + LANDMARKS + part * LANES, LANES)
            packs[i, rows] = mark_v[:, part * LANES : (part + 1) * LANES]
        two = [
            pltpu.make_async_copy(packs.at[i], near[i], out_sems.at[i, 0]),
            pltpu.make_async_copy(packs.at[i, pl.ds(frames, 2 * LANDMARKS)], far[i], out_sems.at[i, 1]),
        ]
        for store in two:
            store.start()
        stores += two
    for store in stores:
        store.wait()


def mark_strips(q, k, v, team, streams, stream, head_dim):
    frames = q.shape[0]
    strips = team
    near = jax.ShapeDtypeStruct((frames + 2 * LANDMARKS, LANES), BF16)
    far = jax.ShapeDtypeStruct((2 * LANDMARKS, LANES), BF16)
    out = pl.pallas_call(
        functools.partial(marks_kernel, team, streams, stream, head_dim),
        out_shape=[near] * strips + [far] * strips,
        in_specs=[HBM] * 3,
        out_specs=[ANY] * (2 * strips),
        scratch_shapes=[
            pltpu.VMEM((strips, frames + 2 * LANDMARKS, LANES), BF16),
            pltpu.VMEM((strips, 2, frames, LANES), BF16),
            pltpu.VMEM((frames, LANDMARKS), F32),
            pltpu.VMEM((frames, LANDMARKS), F32),
            pltpu.SemaphoreType.DMA((strips, 3)),
            pltpu.SemaphoreType.DMA((strips, 2)),
        ],
        compiler_params=pltpu.CompilerParams(vmem_limit_bytes=60 << 20),
    )(q, k, v)
    return out[:strips], out[strips:]


def head_queries(block, head_dim):
    flat = block.astype(F32).T.astype(BF16)
    parts = []
    for low in range(0, LANES, head_dim):
        pieces = [jnp.zeros((low, flat.shape[1]), BF16), flat[low : low + head_dim]]
        pieces.append(jnp.zeros((LANES - low - head_dim, flat.shape[1]), BF16))
        parts.append(jnp.concatenate([piece for piece in pieces if piece.shape[0]], axis=0))
    return parts


def mark_keys_of(ref, base):
    return ref[pl.ds(base, LANDMARKS)]


def mark_values_of(ref, base, h, head_dim):
    parts = [
        ref[pl.ds(base + LANDMARKS + part * LANES + h * head_dim, head_dim)] for part in range(LANDMARKS // LANES)
    ]
    return jnp.concatenate([jnp.concatenate(parts, axis=1), jnp.ones((ONES, LANDMARKS), BF16)], axis=0)


def query_items(frames, head_dim, dests):
    return [(n, b, h) for n in range(dests) for b in range(frames // QUERY_BLOCK) for h in range(LANES // head_dim)]


def gather_sums(queries, sources, weights, head_dim, dests, frames, done):
    scale = head_dim**-0.5 * math.log2(math.e)
    items = query_items(frames, head_dim, dests)
    for i in range(len(items) + 1):
        if i < len(items):
            n, b, h = items[i]
            if h == 0:
                heads = head_queries(queries[n][pl.ds(b * QUERY_BLOCK, QUERY_BLOCK)], head_dim)
            query = heads[h]
        for c, (ref, base) in enumerate(sources):
            rows = pl.ds(c * LANDMARKS, LANDMARKS)
            if i < len(items):
                weights[i % 2][rows] = jnp.exp2(dot(mark_keys_of(ref, base), query) * scale).astype(BF16)
            if i > 0:
                part = dot(mark_values_of(ref, base, items[i - 1][2], head_dim), weights[1 - i % 2][rows])
                sums = part if c == 0 else sums + part
        if i > 0:
            done(items[i - 1], sums)


def near_kernel(team, frames, head_dim, *refs):
    near, partial, weights = refs[:team], refs[team], refs[team + 1 :]

    def done(item, sums):
        n, b, h = item
        partial[n, h, :, pl.ds(b * QUERY_BLOCK, QUERY_BLOCK)] = sums

    gather_sums(near, [(ref, frames) for ref in near], weights, head_dim, team, frames, done)


def mix_near(near, frames, head_dim):
    team, strip_heads = len(near), LANES // head_dim
    return pl.pallas_call(
        functools.partial(near_kernel, team, frames, head_dim),
        out_shape=jax.ShapeDtypeStruct((team, strip_heads, head_dim + ONES, frames), F32),
        in_specs=[VMEM] * team,
        out_specs=VMEM,
        scratch_shapes=[pltpu.VMEM((team * LANDMARKS, QUERY_BLOCK), BF16)] * 2,
        compiler_params=pltpu.CompilerParams(vmem_limit_bytes=16 << 20),
    )(*near)


def far_kernel(team, sources, dests, frames, head_dim, partial, *refs):
    near, far = refs[:team], refs[team:sources]
    outs = refs[sources : sources + len(dests)]
    weight_a, weight_b, scores, all_keys, all_values, held = refs[sources + len(dests) :]
    strip_heads = LANES // head_dim
    scale = head_dim**-0.5 * math.log2(math.e)
    bounds = [jnp.full((1, QUERY_BLOCK), 1.0, F32)] * 2
    heads = []

    def done(item, sums):
        n, b, h = item
        columns = pl.ds(b * QUERY_BLOCK, QUERY_BLOCK)
        sums = sums + partial[dests[n], h, :, columns]
        total = sums[head_dim : head_dim + 1]
        bounds[:] = [jnp.minimum(bounds[0], total), jnp.maximum(bounds[1], total)]
        heads.append(sums[:head_dim] / total)
        if h == strip_heads - 1:
            outs[n][columns] = jnp.concatenate(heads, axis=0).T.astype(BF16)
            heads.clear()

    queries = [near[d] for d in dests]
    gather_sums(queries, [(ref, 0) for ref in far], (weight_a, weight_b), head_dim, len(dests), frames, done)
    unsafe = jnp.sum(jnp.where((bounds[0] > 2.0**-40) & (bounds[1] < 2.0**100), 0, 1))

    @pl.when(unsafe > 0)
    def _():
        everything = [(ref, frames) for ref in near] + [(ref, 0) for ref in far]
        for c, (ref, base) in enumerate(everything):
            all_keys[pl.ds(c * LANDMARKS, LANDMARKS)] = mark_keys_of(ref, base)
            for h in range(strip_heads):
                all_values[h * sources + c] = mark_values_of(ref, base, h, head_dim)
        lane = lax.broadcasted_iota(jnp.int32, (QUERY_BLOCK, LANES), 1)
        for n, d in enumerate(dests):

            def exact(i, carry):
                b, h = i // strip_heads, i % strip_heads
                block = pl.ds(pl.multiple_of(b * QUERY_BLOCK, QUERY_BLOCK), QUERY_BLOCK)
                own = (lane >= h * head_dim) & (lane < (h + 1) * head_dim)
                query = jnp.where(own, near[d][block].astype(F32), 0.0).T.astype(BF16)

                def rows_of(c):
                    return pl.ds(pl.multiple_of(c * LANDMARKS, LANDMARKS), LANDMARKS)

                def score(c, top):
                    part = dot(all_keys[rows_of(c)], query)
                    scores[rows_of(c)] = part
                    return jnp.maximum(top, jnp.max(part, axis=0, keepdims=True))

                top = lax.fori_loop(0, sources, score, jnp.full((1, QUERY_BLOCK), -jnp.inf, F32))

                def mix(c, sums):
                    weight = jnp.exp2((scores[rows_of(c)] - top) * scale).astype(BF16)
                    return sums + dot(all_values[h * sources + c], weight)

                sums = lax.fori_loop(0, sources, mix, jnp.zeros((head_dim + ONES, QUERY_BLOCK), F32))
                held[pl.ds(pl.multiple_of(h * head_dim, head_dim), head_dim)] = sums[:head_dim] / sums[head_dim : head_dim + 1]

                @pl.when(h == strip_heads - 1)
                def _():
                    outs[n][block] = held[...].T.astype(BF16)

                return carry

            lax.fori_loop(0, frames // QUERY_BLOCK * strip_heads, exact, 0)


def mix_far(partial, near, far, dests, frames, head_dim):
    team, sources = len(near), len(near) + len(far)
    return pl.pallas_call(
        functools.partial(far_kernel, team, sources, dests, frames, head_dim),
        out_shape=[jax.ShapeDtypeStruct((frames, LANES), BF16)] * len(dests),
        in_specs=[VMEM] * (1 + sources),
        out_specs=[VMEM] * len(dests),
        scratch_shapes=[
            pltpu.VMEM((len(far) * LANDMARKS, QUERY_BLOCK), BF16),
            pltpu.VMEM((len(far) * LANDMARKS, QUERY_BLOCK), BF16),
            pltpu.VMEM((sources * LANDMARKS, QUERY_BLOCK), F32),
            pltpu.VMEM((sources * LANDMARKS, LANES), BF16),
            pltpu.VMEM((LANES // head_dim * sources, head_dim + ONES, LANDMARKS), BF16),
            pltpu.VMEM((LANES, QUERY_BLOCK), F32),
        ],
        compiler_params=pltpu.CompilerParams(vmem_limit_bytes=24 << 20),
    )(partial, *near, *far)


def finish_kernel(team, streams, packs, blocks, owners, bases, offsets, w_out, gain, *refs):
    strips = refs[: team * streams]
    encoded = refs[team * streams]
    sends = refs[team * streams + 1 :]
    me = lax.axis_index("tm") % team
    my_pack = lax.axis_index("pack")
    width = streams * LANES
    model = w_out.shape[1]
    slots = packs * SLOTS * WINDOW
    owner = [owners[b, 0] for b in range(blocks)]
    starts = []
    for b in range(blocks):
        rank = jnp.int32(0)
        for a in range(b):
            rank = rank + jnp.where(owner[a] == owner[b], 1, 0)
        starts.append((jnp.bitwise_xor(owner[b], my_pack) * SLOTS + rank) * WINDOW)
    slot_row = lax.broadcasted_iota(jnp.int32, (slots, BLOCK), 0)
    slot_lane = lax.broadcasted_iota(jnp.int32, (1, slots), 1)
    hits, rows_to = [], jnp.zeros((1, slots), jnp.int32)
    for b in range(blocks):
        hits.append((slot_row == offsets[pl.ds(b, 1)] + starts[b]).astype(F32).astype(BF16))
        step = slot_lane - starts[b]
        rows_to = rows_to + jnp.where((step >= 0) & (step < WINDOW), step + (bases[0, b] + 1), 0)
    hit = jnp.concatenate(hits, axis=1)
    frame_counts = lax.dot_general(
        jnp.ones((META, blocks * BLOCK), BF16), hit, (((1,), (1,)), ((), ())), preferred_element_type=F32
    )
    for b in range(blocks):
        rows = pl.ds(b * BLOCK, BLOCK)
        projected = None
        for d in range(team):
            strip = jnp.concatenate([strips[s * team + d][rows] for s in range(streams)], axis=1)
            first = pl.multiple_of(jnp.bitwise_xor(me, d) * width, LANES)
            part = dot(strip, w_out[pl.ds(first, width)])
            projected = part if projected is None else projected + part
        power = jnp.mean(projected * projected, axis=-1, keepdims=True)
        encoded[rows] = (projected * lax.rsqrt(power + 1e-06) * gain[...]).astype(BF16)
    sums = dot(hit, encoded[...]).astype(BF16)
    meta_row = lax.broadcasted_iota(jnp.int32, (META, slots), 0)
    meta = jnp.where(meta_row == 0, rows_to.astype(F32), jnp.where(meta_row == 1, frame_counts, 0.0))
    part = SLOTS * WINDOW
    for e in range(packs):
        sends[e][pl.ds(0, part)] = sums[e * part : (e + 1) * part]
        sends[e][pl.ds(part, META)] = jnp.zeros((META, model), BF16)
        sends[e][pl.ds(part, META), pl.ds(0, slots)] = meta.astype(BF16)


def finish(strips, w_out, gain, owners, bases, offsets, team, streams, packs):
    frames, model = strips[0].shape[0], w_out.shape[1]
    blocks = owners.shape[0]
    send = jax.ShapeDtypeStruct((SLOTS * WINDOW + META, model), BF16)
    out = pl.pallas_call(
        functools.partial(finish_kernel, team, streams, packs, blocks),
        out_shape=[jax.ShapeDtypeStruct((frames, model), BF16)] + [send] * packs,
        in_specs=[SMEM, SMEM] + [VMEM] * (3 + len(strips)),
        out_specs=[VMEM] * (1 + packs),
        compiler_params=pltpu.CompilerParams(vmem_limit_bytes=24 << 20),
        name="finish",
    )(owners, bases, offsets, w_out, gain, *strips)
    return out[0], out[1:]


def pool_kernel(packs, *refs):
    got, pooled = refs[:packs], refs[packs]
    part = SLOTS * WINDOW
    slots = packs * part
    lane = lax.broadcasted_iota(jnp.int32, (1, slots), 1)
    rows_to, counts = jnp.zeros((1, slots), F32), jnp.zeros((1, slots), F32)
    for e in range(packs):
        meta = got[e][pl.ds(part, META), pl.ds(0, slots)].astype(F32)
        mine = (lane >= e * part) & (lane < (e + 1) * part)
        rows_to = jnp.where(mine, meta[0:1], rows_to)
        counts = jnp.where(mine, meta[1:2], counts)
    row = lax.broadcasted_iota(jnp.int32, (POOL_DEV, slots), 0)
    place = row + 1 == rows_to.astype(jnp.int32)
    total = jnp.sum(jnp.where(place, counts, 0.0), axis=1, keepdims=True)
    rows = jnp.concatenate([got[e][pl.ds(0, part)] for e in range(packs)], axis=0)
    sums = dot(place.astype(F32).astype(BF16), rows)
    pooled[...] = (sums / jnp.maximum(total, 1.0)).astype(BF16)


def pool(got):
    return pl.pallas_call(
        functools.partial(pool_kernel, len(got)),
        out_shape=jax.ShapeDtypeStruct((POOL_DEV, got[0].shape[1]), BF16),
        in_specs=[VMEM] * len(got),
        out_specs=VMEM,
        compiler_params=pltpu.CompilerParams(vmem_limit_bytes=8 << 20),
        name="pool",
    )(*got)


def swap(array, axis, size, bits):
    return lax.ppermute(array, axis, [(i, i ^ bits) for i in range(size)])


def local(team, queries, keys, values, w_out, norm_gain, block_owner, block_base, frame_offset):
    q, k, v = queries[0], keys[0], values[0]
    frames, model = q.shape
    tm, packs = lax.axis_size("tm"), lax.axis_size("pack")
    head_dim = model // HEADS
    streams = model // team // LANES
    near, far, partial, strips = [], [], [], []
    for s in range(streams):
        near_out, far_out = mark_strips(q, k, v, team, streams, s, head_dim)
        far.append([swap(far_out[d], "tm", tm, other + d) for other in range(team, tm, team) for d in range(team)])
        near.append([near_out[0]] + [swap(near_out[d], "tm", tm, d) for d in range(1, team)])
    for s in range(streams):
        partial.append(mix_near(near[s], frames, head_dim))
    for s in range(streams):
        mixed = {}
        for dests in turns_of(team, streams, s):
            mixed.update(zip(dests, mix_far(partial[s], near[s], far[s], dests, frames, head_dim)))
        strips += [mixed[0]] + [swap(mixed[d], "tm", tm, d) for d in range(1, team)]
    encoded, sends = finish(
        strips, w_out, norm_gain[None], block_owner[0], block_base, frame_offset[0], team, streams, packs
    )
    got = [sends[0]] + [swap(sends[e], "pack", packs, e) for e in range(1, packs)]
    return encoded[None], pool(got)[None]


def turns_of(team, streams, stream):
    dests = list(reversed(range(team)))
    return [dests] if stream < streams - 1 or team < 4 else [dests[:-2], dests[-2:]]


def solution(mesh):
    tm = mesh.shape["tm"]
    team = tm // 2
    return jax.shard_map(
        functools.partial(local, team),
        mesh=mesh,
        in_specs=(
            P("pack", "tm", None),
            P("pack", "tm", None),
            P("pack", "tm", None),
            P(),
            P(),
            P("pack", "tm", None),
            P("pack", "tm"),
            P("pack", "tm", None),
        ),
        out_specs=(P("pack", "tm", None), P("pack", "tm", None)),
        check_vma=False,
    )
```

```python
import functools
import math

import jax
import jax.numpy as jnp
from jax import lax
from jax.experimental import pallas as pl
from jax.experimental.pallas import tpu as pltpu
from jax.sharding import PartitionSpec as P


HEADS = 16
LANDMARKS = 256
BLOCK = 128
POOL_DEV = 128
WINDOW = 16
LANES = 128
ONES = 16
SLOTS = 2
QUERY_BLOCK = 256
BF16 = jnp.bfloat16
F32 = jnp.float32


ANY = pl.BlockSpec(memory_space=pl.ANY)
HBM = pl.BlockSpec(memory_space=pltpu.HBM)
VMEM = pl.BlockSpec(memory_space=pltpu.VMEM)
SMEM = pl.BlockSpec(memory_space=pltpu.SMEM)


def dot(a, b):
    return jnp.dot(a, b, preferred_element_type=F32)


def marks_kernel(team, streams, stream, head_dim, q_hbm, k_hbm, v_hbm, *refs):
    frames = q_hbm.shape[0]
    strips = team
    near, far = refs[:strips], refs[strips : 2 * strips]
    packs, ins, score_a, score_b, in_sems, out_sems = refs[2 * strips :]
    me = lax.axis_index("tm") % team
    span = frames // LANDMARKS
    strip_heads = LANES // head_dim
    scale = head_dim**-0.5 * math.log2(math.e)
    loads = []
    for i in range(strips):
        column = pl.multiple_of((jnp.bitwise_xor(me, i) * streams + stream) * LANES, LANES)
        columns = pl.ds(column, LANES)
        three = [
            pltpu.make_async_copy(q_hbm.at[:, columns], packs.at[i, pl.ds(0, frames)], in_sems.at[i, 0]),
            pltpu.make_async_copy(k_hbm.at[:, columns], ins.at[i, 0], in_sems.at[i, 1]),
            pltpu.make_async_copy(v_hbm.at[:, columns], ins.at[i, 1], in_sems.at[i, 2]),
        ]
        for load in three:
            load.start()
        loads.append(three)
    row = lax.broadcasted_iota(jnp.int32, (LANDMARKS, frames), 0)
    frame = lax.broadcasted_iota(jnp.int32, (LANDMARKS, frames), 1)
    member = ((frame >= row * span) & (frame < (row + 1) * span)).astype(BF16)
    lane_row = lax.broadcasted_iota(jnp.int32, (LANES, LANDMARKS), 0)
    ones = jnp.ones((ONES, frames), BF16)
    scores = (score_a, score_b)
    stores = []

    def prepare(i):
        for load in loads[i]:
            load.wait()
        mark_q = (dot(member, packs[i, pl.ds(0, frames)]) * (1.0 / span)).astype(BF16).astype(F32).T
        mark_k = (dot(member, ins[i, 0]) * (1.0 / span)).astype(BF16)
        packs[i, pl.ds(frames, LANDMARKS)] = mark_k
        return mark_q, ins[i, 1].astype(F32).T.astype(BF16)

    def score(i, h, slot, mark_q):
        low = h * head_dim
        own = jnp.where((lane_row >= low) & (lane_row < low + head_dim), mark_q, 0.0).astype(BF16)
        part = dot(ins[i, 0], own)
        scores[slot][...] = part
        return jnp.max(part, axis=0, keepdims=True)

    items = [(i, h) for i in range(strips) for h in range(strip_heads)]
    mark_q, v_next = prepare(0)
    top, heads = score(0, 0, 0, mark_q), []
    for n, (i, h) in enumerate(items):
        slot, most, v_t = n % 2, top, v_next
        if n + 1 < len(items):
            j, g = items[n + 1]
            if g == 0:
                mark_q, v_next = prepare(j)
            top = score(j, g, 1 - slot, mark_q)
        weights = jnp.exp2((scores[slot][...] - most) * scale).astype(BF16)
        mixed = dot(jnp.concatenate([v_t[h * head_dim : (h + 1) * head_dim], ones], axis=0), weights)
        heads.append(mixed[:head_dim] / mixed[head_dim : head_dim + 1])
        if h < strip_heads - 1:
            continue
        mark_v, heads = jnp.concatenate(heads, axis=0).astype(BF16), []
        for part in range(LANDMARKS // LANES):
            rows = pl.ds(frames + LANDMARKS + part * LANES, LANES)
            packs[i, rows] = mark_v[:, part * LANES : (part + 1) * LANES]
        two = [
            pltpu.make_async_copy(packs.at[i], near[i], out_sems.at[i, 0]),
            pltpu.make_async_copy(packs.at[i, pl.ds(frames, 2 * LANDMARKS)], far[i], out_sems.at[i, 1]),
        ]
        for store in two:
            store.start()
        stores += two
    for store in stores:
        store.wait()


def mark_strips(q, k, v, team, streams, stream, head_dim):
    frames = q.shape[0]
    strips = team
    near = jax.ShapeDtypeStruct((frames + 2 * LANDMARKS, LANES), BF16)
    far = jax.ShapeDtypeStruct((2 * LANDMARKS, LANES), BF16)
    out = pl.pallas_call(
        functools.partial(marks_kernel, team, streams, stream, head_dim),
        out_shape=[near] * strips + [far] * strips,
        in_specs=[HBM] * 3,
        out_specs=[ANY] * (2 * strips),
        scratch_shapes=[
            pltpu.VMEM((strips, frames + 2 * LANDMARKS, LANES), BF16),
            pltpu.VMEM((strips, 2, frames, LANES), BF16),
            pltpu.VMEM((frames, LANDMARKS), F32),
            pltpu.VMEM((frames, LANDMARKS), F32),
            pltpu.SemaphoreType.DMA((strips, 3)),
            pltpu.SemaphoreType.DMA((strips, 2)),
        ],
        compiler_params=pltpu.CompilerParams(vmem_limit_bytes=60 << 20),
    )(q, k, v)
    return out[:strips], out[strips:]


def head_queries(block, head_dim):
    flat = block.astype(F32).T.astype(BF16)
    parts = []
    for low in range(0, LANES, head_dim):
        pieces = [jnp.zeros((low, flat.shape[1]), BF16), flat[low : low + head_dim]]
        pieces.append(jnp.zeros((LANES - low - head_dim, flat.shape[1]), BF16))
        parts.append(jnp.concatenate([piece for piece in pieces if piece.shape[0]], axis=0))
    return parts


def mark_keys_of(ref, base):
    return ref[pl.ds(base, LANDMARKS)]


def mark_values_of(ref, base, h, head_dim):
    parts = [
        ref[pl.ds(base + LANDMARKS + part * LANES + h * head_dim, head_dim)] for part in range(LANDMARKS // LANES)
    ]
    return jnp.concatenate([jnp.concatenate(parts, axis=1), jnp.ones((ONES, LANDMARKS), BF16)], axis=0)


def query_items(frames, head_dim, dests):
    return [(n, b, h) for n in range(dests) for b in range(frames // QUERY_BLOCK) for h in range(LANES // head_dim)]


def gather_sums(queries, sources, weights, head_dim, dests, frames, done):
    scale = head_dim**-0.5 * math.log2(math.e)
    items = query_items(frames, head_dim, dests)
    for i in range(len(items) + 1):
        if i < len(items):
            n, b, h = items[i]
            if h == 0:
                heads = head_queries(queries[n][pl.ds(b * QUERY_BLOCK, QUERY_BLOCK)], head_dim)
            query = heads[h]
        for c, (ref, base) in enumerate(sources):
            rows = pl.ds(c * LANDMARKS, LANDMARKS)
            if i < len(items):
                weights[i % 2][rows] = jnp.exp2(dot(mark_keys_of(ref, base), query) * scale).astype(BF16)
            if i > 0:
                part = dot(mark_values_of(ref, base, items[i - 1][2], head_dim), weights[1 - i % 2][rows])
                sums = part if c == 0 else sums + part
        if i > 0:
            done(items[i - 1], sums)


def near_kernel(team, frames, head_dim, *refs):
    near, partial, weights = refs[:team], refs[team], refs[team + 1 :]

    def done(item, sums):
        n, b, h = item
        partial[n, h, :, pl.ds(b * QUERY_BLOCK, QUERY_BLOCK)] = sums

    gather_sums(near, [(ref, frames) for ref in near], weights, head_dim, team, frames, done)


def mix_near(near, frames, head_dim):
    team, strip_heads = len(near), LANES // head_dim
    return pl.pallas_call(
        functools.partial(near_kernel, team, frames, head_dim),
        out_shape=jax.ShapeDtypeStruct((team, strip_heads, head_dim + ONES, frames), F32),
        in_specs=[VMEM] * team,
        out_specs=VMEM,
        scratch_shapes=[pltpu.VMEM((team * LANDMARKS, QUERY_BLOCK), BF16)] * 2,
        compiler_params=pltpu.CompilerParams(vmem_limit_bytes=16 << 20),
    )(*near)


def far_kernel(team, sources, frames, head_dim, partial, *refs):
    near, far = refs[:team], refs[team:sources]
    outs = refs[sources : sources + team]
    weight_a, weight_b, scores, all_keys, all_values, held = refs[sources + team :]
    strip_heads = LANES // head_dim
    scale = head_dim**-0.5 * math.log2(math.e)
    bounds = [jnp.full((1, QUERY_BLOCK), 1.0, F32)] * 2
    heads = []

    def done(item, sums):
        n, b, h = item
        columns = pl.ds(b * QUERY_BLOCK, QUERY_BLOCK)
        sums = sums + partial[n, h, :, columns]
        total = sums[head_dim : head_dim + 1]
        bounds[:] = [jnp.minimum(bounds[0], total), jnp.maximum(bounds[1], total)]
        heads.append(sums[:head_dim] / total)
        if h == strip_heads - 1:
            outs[n][columns] = jnp.concatenate(heads, axis=0).T.astype(BF16)
            heads.clear()

    gather_sums(near, [(ref, 0) for ref in far], (weight_a, weight_b), head_dim, team, frames, done)
    unsafe = jnp.sum(jnp.where((bounds[0] > 2.0**-40) & (bounds[1] < 2.0**100), 0, 1))

    @pl.when(unsafe > 0)
    def _():
        everything = [(ref, frames) for ref in near] + [(ref, 0) for ref in far]
        for c, (ref, base) in enumerate(everything):
            all_keys[pl.ds(c * LANDMARKS, LANDMARKS)] = mark_keys_of(ref, base)
            for h in range(strip_heads):
                all_values[h * sources + c] = mark_values_of(ref, base, h, head_dim)
        lane = lax.broadcasted_iota(jnp.int32, (QUERY_BLOCK, LANES), 1)
        for n in range(team):

            def exact(i, carry):
                b, h = i // strip_heads, i % strip_heads
                block = pl.ds(pl.multiple_of(b * QUERY_BLOCK, QUERY_BLOCK), QUERY_BLOCK)
                own = (lane >= h * head_dim) & (lane < (h + 1) * head_dim)
                query = jnp.where(own, near[n][block].astype(F32), 0.0).T.astype(BF16)

                def rows_of(c):
                    return pl.ds(pl.multiple_of(c * LANDMARKS, LANDMARKS), LANDMARKS)

                def score(c, top):
                    part = dot(all_keys[rows_of(c)], query)
                    scores[rows_of(c)] = part
                    return jnp.maximum(top, jnp.max(part, axis=0, keepdims=True))

                top = lax.fori_loop(0, sources, score, jnp.full((1, QUERY_BLOCK), -jnp.inf, F32))

                def mix(c, sums):
                    weight = jnp.exp2((scores[rows_of(c)] - top) * scale).astype(BF16)
                    return sums + dot(all_values[h * sources + c], weight)

                sums = lax.fori_loop(0, sources, mix, jnp.zeros((head_dim + ONES, QUERY_BLOCK), F32))
                held[pl.ds(pl.multiple_of(h * head_dim, head_dim), head_dim)] = sums[:head_dim] / sums[head_dim : head_dim + 1]

                @pl.when(h == strip_heads - 1)
                def _():
                    outs[n][block] = held[...].T.astype(BF16)

                return carry

            lax.fori_loop(0, frames // QUERY_BLOCK * strip_heads, exact, 0)


def mix_far(partial, near, far, frames, head_dim):
    team, sources = len(near), len(near) + len(far)
    return pl.pallas_call(
        functools.partial(far_kernel, team, sources, frames, head_dim),
        out_shape=[jax.ShapeDtypeStruct((frames, LANES), BF16)] * team,
        in_specs=[VMEM] * (1 + sources),
        out_specs=[VMEM] * team,
        scratch_shapes=[
            pltpu.VMEM((len(far) * LANDMARKS, QUERY_BLOCK), BF16),
            pltpu.VMEM((len(far) * LANDMARKS, QUERY_BLOCK), BF16),
            pltpu.VMEM((sources * LANDMARKS, QUERY_BLOCK), F32),
            pltpu.VMEM((sources * LANDMARKS, LANES), BF16),
            pltpu.VMEM((LANES // head_dim * sources, head_dim + ONES, LANDMARKS), BF16),
            pltpu.VMEM((LANES, QUERY_BLOCK), F32),
        ],
        compiler_params=pltpu.CompilerParams(vmem_limit_bytes=24 << 20),
    )(partial, *near, *far)


def finish_kernel(team, streams, packs, blocks, owners, bases, offsets, w_out, gain, *refs):
    strips = refs[: team * streams]
    encoded = refs[team * streams]
    sends = refs[team * streams + 1 :]
    me = lax.axis_index("tm") % team
    my_pack = lax.axis_index("pack")
    width = streams * LANES
    model = w_out.shape[1]
    slots = packs * SLOTS * WINDOW
    owner = [owners[b, 0] for b in range(blocks)]
    starts = []
    for b in range(blocks):
        rank = jnp.int32(0)
        for a in range(b):
            rank = rank + jnp.where(owner[a] == owner[b], 1, 0)
        starts.append((jnp.bitwise_xor(owner[b], my_pack) * SLOTS + rank) * WINDOW)
    slot_row = lax.broadcasted_iota(jnp.int32, (slots, BLOCK), 0)
    slot_lane = lax.broadcasted_iota(jnp.int32, (1, slots), 1)
    hits, rows_to = [], jnp.zeros((1, slots), jnp.int32)
    for b in range(blocks):
        hits.append((slot_row == offsets[pl.ds(b, 1)] + starts[b]).astype(F32).astype(BF16))
        step = slot_lane - starts[b]
        rows_to = rows_to + jnp.where((step >= 0) & (step < WINDOW), step + (bases[0, b] + 1), 0)
    hit = jnp.concatenate(hits, axis=1)
    frame_counts = lax.dot_general(
        jnp.ones((SLOTS * WINDOW, blocks * BLOCK), BF16), hit, (((1,), (1,)), ((), ())), preferred_element_type=F32
    )
    for b in range(blocks):
        rows = pl.ds(b * BLOCK, BLOCK)
        projected = None
        for d in range(team):
            strip = jnp.concatenate([strips[s * team + d][rows] for s in range(streams)], axis=1)
            first = pl.multiple_of(jnp.bitwise_xor(me, d) * width, LANES)
            part = dot(strip, w_out[pl.ds(first, width)])
            projected = part if projected is None else projected + part
        power = jnp.mean(projected * projected, axis=-1, keepdims=True)
        encoded[rows] = (projected * lax.rsqrt(power + 1e-06) * gain[...]).astype(BF16)
    sums = dot(hit, encoded[...]).astype(BF16)
    part = SLOTS * WINDOW
    meta_row = lax.broadcasted_iota(jnp.int32, (part, slots), 0)
    meta = jnp.where(meta_row == 0, rows_to.astype(F32), jnp.where(meta_row == 1, frame_counts, 0.0))
    for e in range(packs):
        sends[e][:, pl.ds(0, model)] = sums[e * part : (e + 1) * part]
        sends[e][:, pl.ds(model, slots)] = meta.astype(BF16)


def finish(strips, w_out, gain, owners, bases, offsets, team, streams, packs):
    frames, model = strips[0].shape[0], w_out.shape[1]
    blocks = owners.shape[0]
    part = SLOTS * WINDOW
    send = jax.ShapeDtypeStruct((part, model + packs * part), BF16)
    out = pl.pallas_call(
        functools.partial(finish_kernel, team, streams, packs, blocks),
        out_shape=[jax.ShapeDtypeStruct((frames, model), BF16)] + [send] * packs,
        in_specs=[SMEM, SMEM] + [VMEM] * (3 + len(strips)),
        out_specs=[VMEM] * (1 + packs),
        compiler_params=pltpu.CompilerParams(vmem_limit_bytes=24 << 20),
        name="finish",
    )(owners, bases, offsets, w_out, gain, *strips)
    return out[0], out[1:]


def pool_kernel(packs, *refs):
    got, pooled = refs[:packs], refs[packs]
    part = SLOTS * WINDOW
    slots = packs * part
    model = pooled.shape[1]
    lane = lax.broadcasted_iota(jnp.int32, (1, slots), 1)
    rows_to, counts = jnp.zeros((1, slots), F32), jnp.zeros((1, slots), F32)
    for e in range(packs):
        meta = got[e][:, pl.ds(model, slots)].astype(F32)
        mine = (lane >= e * part) & (lane < (e + 1) * part)
        rows_to = jnp.where(mine, meta[0:1], rows_to)
        counts = jnp.where(mine, meta[1:2], counts)
    row = lax.broadcasted_iota(jnp.int32, (POOL_DEV, slots), 0)
    place = row + 1 == rows_to.astype(jnp.int32)
    total = jnp.sum(jnp.where(place, counts, 0.0), axis=1, keepdims=True)
    rows = jnp.concatenate([got[e][:, pl.ds(0, model)] for e in range(packs)], axis=0)
    sums = dot(place.astype(F32).astype(BF16), rows)
    pooled[...] = (sums / jnp.maximum(total, 1.0)).astype(BF16)


def pool(got):
    return pl.pallas_call(
        functools.partial(pool_kernel, len(got)),
        out_shape=jax.ShapeDtypeStruct((POOL_DEV, got[0].shape[1] - len(got) * SLOTS * WINDOW), BF16),
        in_specs=[VMEM] * len(got),
        out_specs=VMEM,
        compiler_params=pltpu.CompilerParams(vmem_limit_bytes=8 << 20),
        name="pool",
    )(*got)


def swap(array, axis, size, bits):
    return lax.ppermute(array, axis, [(i, i ^ bits) for i in range(size)])


def local(team, queries, keys, values, w_out, norm_gain, block_owner, block_base, frame_offset):
    q, k, v = queries[0], keys[0], values[0]
    frames, model = q.shape
    tm, packs = lax.axis_size("tm"), lax.axis_size("pack")
    head_dim = model // HEADS
    streams = model // team // LANES
    near, far, partial, strips = [], [], [], []
    for s in range(streams):
        near_out, far_out = mark_strips(q, k, v, team, streams, s, head_dim)
        far.append([swap(far_out[d], "tm", tm, other + d) for other in range(team, tm, team) for d in range(team)])
        near.append([near_out[0]] + [swap(near_out[d], "tm", tm, d) for d in range(1, team)])
    for s in range(streams):
        partial.append(mix_near(near[s], frames, head_dim))
    for s in range(streams):
        mixed = mix_far(partial[s], near[s], far[s], frames, head_dim)
        strips += [mixed[0]] + [swap(mixed[d], "tm", tm, d) for d in range(1, team)]
    encoded, sends = finish(
        strips, w_out, norm_gain[None], block_owner[0], block_base, frame_offset[0], team, streams, packs
    )
    got = [sends[0]] + [swap(sends[e], "pack", packs, e) for e in range(1, packs)]
    return encoded[None], pool(got)[None]


def solution(mesh):
    tm = mesh.shape["tm"]
    team = tm // 2
    return jax.shard_map(
        functools.partial(local, team),
        mesh=mesh,
        in_specs=(
            P("pack", "tm", None),
            P("pack", "tm", None),
            P("pack", "tm", None),
            P(),
            P(),
            P("pack", "tm", None),
            P("pack", "tm"),
            P("pack", "tm", None),
        ),
        out_specs=(P("pack", "tm", None), P("pack", "tm", None)),
        check_vma=False,
    )
```

```python
import functools
import math

import jax
import jax.numpy as jnp
from jax import lax
from jax.experimental import pallas as pl
from jax.experimental.pallas import tpu as pltpu
from jax.sharding import PartitionSpec as P


HEADS = 16
LANDMARKS = 256
BLOCK = 128
POOL_DEV = 128
WINDOW = 16
LANES = 128
ONES = 16
SLOTS = 2
QUERY_BLOCK = 256
BF16 = jnp.bfloat16
F32 = jnp.float32


ANY = pl.BlockSpec(memory_space=pl.ANY)
HBM = pl.BlockSpec(memory_space=pltpu.HBM)
VMEM = pl.BlockSpec(memory_space=pltpu.VMEM)
SMEM = pl.BlockSpec(memory_space=pltpu.SMEM)


def dot(a, b):
    return jnp.dot(a, b, preferred_element_type=F32)


def marks_kernel(team, streams, stream, dests, head_dim, q_hbm, k_hbm, v_hbm, *refs):
    frames = q_hbm.shape[0]
    strips = len(dests)
    near, far = refs[:strips], refs[strips : 2 * strips]
    packs, ins, score_a, score_b, in_sems, out_sems = refs[2 * strips :]
    me = lax.axis_index("tm") % team
    span = frames // LANDMARKS
    strip_heads = LANES // head_dim
    scale = head_dim**-0.5 * math.log2(math.e)
    loads = []
    for i in range(strips):
        column = pl.multiple_of((jnp.bitwise_xor(me, dests[i]) * streams + stream) * LANES, LANES)
        columns = pl.ds(column, LANES)
        three = [
            pltpu.make_async_copy(q_hbm.at[:, columns], packs.at[i, pl.ds(0, frames)], in_sems.at[i, 0]),
            pltpu.make_async_copy(k_hbm.at[:, columns], ins.at[i, 0], in_sems.at[i, 1]),
            pltpu.make_async_copy(v_hbm.at[:, columns], ins.at[i, 1], in_sems.at[i, 2]),
        ]
        for load in three:
            load.start()
        loads.append(three)
    row = lax.broadcasted_iota(jnp.int32, (LANDMARKS, frames), 0)
    frame = lax.broadcasted_iota(jnp.int32, (LANDMARKS, frames), 1)
    member = ((frame >= row * span) & (frame < (row + 1) * span)).astype(BF16)
    lane_row = lax.broadcasted_iota(jnp.int32, (LANES, LANDMARKS), 0)
    ones = jnp.ones((ONES, frames), BF16)
    scores = (score_a, score_b)
    stores = []

    def prepare(i):
        for load in loads[i]:
            load.wait()
        mark_q = (dot(member, packs[i, pl.ds(0, frames)]) * (1.0 / span)).astype(BF16).astype(F32).T
        mark_k = (dot(member, ins[i, 0]) * (1.0 / span)).astype(BF16)
        packs[i, pl.ds(frames, LANDMARKS)] = mark_k
        return mark_q, ins[i, 1].astype(F32).T.astype(BF16)

    def score(i, h, slot, mark_q):
        low = h * head_dim
        own = jnp.where((lane_row >= low) & (lane_row < low + head_dim), mark_q, 0.0).astype(BF16)
        part = dot(ins[i, 0], own)
        scores[slot][...] = part
        return jnp.max(part, axis=0, keepdims=True)

    items = [(i, h) for i in range(strips) for h in range(strip_heads)]
    mark_q, v_next = prepare(0)
    top, heads = score(0, 0, 0, mark_q), []
    for n, (i, h) in enumerate(items):
        slot, most, v_t = n % 2, top, v_next
        if n + 1 < len(items):
            j, g = items[n + 1]
            if g == 0:
                mark_q, v_next = prepare(j)
            top = score(j, g, 1 - slot, mark_q)
        weights = jnp.exp2((scores[slot][...] - most) * scale).astype(BF16)
        mixed = dot(jnp.concatenate([v_t[h * head_dim : (h + 1) * head_dim], ones], axis=0), weights)
        heads.append(mixed[:head_dim] / mixed[head_dim : head_dim + 1])
        if h < strip_heads - 1:
            continue
        mark_v, heads = jnp.concatenate(heads, axis=0).astype(BF16), []
        for part in range(LANDMARKS // LANES):
            rows = pl.ds(frames + LANDMARKS + part * LANES, LANES)
            packs[i, rows] = mark_v[:, part * LANES : (part + 1) * LANES]
        two = [
            pltpu.make_async_copy(packs.at[i], near[i], out_sems.at[i, 0]),
            pltpu.make_async_copy(packs.at[i, pl.ds(frames, 2 * LANDMARKS)], far[i], out_sems.at[i, 1]),
        ]
        for store in two:
            store.start()
        stores += two
    for store in stores:
        store.wait()


def mark_strips(q, k, v, team, streams, stream, dests, head_dim):
    frames = q.shape[0]
    strips = len(dests)
    near = jax.ShapeDtypeStruct((frames + 2 * LANDMARKS, LANES), BF16)
    far = jax.ShapeDtypeStruct((2 * LANDMARKS, LANES), BF16)
    out = pl.pallas_call(
        functools.partial(marks_kernel, team, streams, stream, dests, head_dim),
        out_shape=[near] * strips + [far] * strips,
        in_specs=[HBM] * 3,
        out_specs=[ANY] * (2 * strips),
        scratch_shapes=[
            pltpu.VMEM((strips, frames + 2 * LANDMARKS, LANES), BF16),
            pltpu.VMEM((strips, 2, frames, LANES), BF16),
            pltpu.VMEM((frames, LANDMARKS), F32),
            pltpu.VMEM((frames, LANDMARKS), F32),
            pltpu.SemaphoreType.DMA((strips, 3)),
            pltpu.SemaphoreType.DMA((strips, 2)),
        ],
        compiler_params=pltpu.CompilerParams(vmem_limit_bytes=60 << 20),
    )(q, k, v)
    return out[:strips], out[strips:]


def head_queries(block, head_dim):
    flat = block.astype(F32).T.astype(BF16)
    parts = []
    for low in range(0, LANES, head_dim):
        pieces = [jnp.zeros((low, flat.shape[1]), BF16), flat[low : low + head_dim]]
        pieces.append(jnp.zeros((LANES - low - head_dim, flat.shape[1]), BF16))
        parts.append(jnp.concatenate([piece for piece in pieces if piece.shape[0]], axis=0))
    return parts


def mark_keys_of(ref, base):
    return ref[pl.ds(base, LANDMARKS)]


def mark_values_of(ref, base, h, head_dim):
    parts = [
        ref[pl.ds(base + LANDMARKS + part * LANES + h * head_dim, head_dim)] for part in range(LANDMARKS // LANES)
    ]
    return jnp.concatenate([jnp.concatenate(parts, axis=1), jnp.ones((ONES, LANDMARKS), BF16)], axis=0)


def query_items(frames, head_dim, dests):
    return [(n, b, h) for n in range(dests) for b in range(frames // QUERY_BLOCK) for h in range(LANES // head_dim)]


def gather_sums(queries, sources, weights, head_dim, dests, frames, done):
    scale = head_dim**-0.5 * math.log2(math.e)
    items = query_items(frames, head_dim, dests)
    for i in range(len(items) + 1):
        if i < len(items):
            n, b, h = items[i]
            if h == 0:
                heads = head_queries(queries[n][pl.ds(b * QUERY_BLOCK, QUERY_BLOCK)], head_dim)
            query = heads[h]
        for c, (ref, base) in enumerate(sources):
            rows = pl.ds(c * LANDMARKS, LANDMARKS)
            if i < len(items):
                weights[i % 2][rows] = jnp.exp2(dot(mark_keys_of(ref, base), query) * scale).astype(BF16)
            if i > 0:
                part = dot(mark_values_of(ref, base, items[i - 1][2], head_dim), weights[1 - i % 2][rows])
                sums = part if c == 0 else sums + part
        if i > 0:
            done(items[i - 1], sums)


def part_kernel(team, sources, base, frames, head_dim, more, *refs):
    queries, marks = refs[:team], refs[team : team + sources]
    before, refs = (refs[team + sources], refs[team + sources + 1 :]) if more else (None, refs[team + sources :])
    partial, weights = refs[0], refs[1:]

    def done(item, sums):
        n, b, h = item
        columns = pl.ds(b * QUERY_BLOCK, QUERY_BLOCK)
        partial[n, h, :, columns] = sums + before[n, h, :, columns] if more else sums

    gather_sums(queries, [(ref, base) for ref in marks], weights, head_dim, team, frames, done)


def mix_part(near, marks, base, before, frames, head_dim):
    team, strip_heads = len(near), LANES // head_dim
    more = before is not None
    operands = [*near, *marks] + ([before] if more else [])
    return pl.pallas_call(
        functools.partial(part_kernel, team, len(marks), base, frames, head_dim, more),
        out_shape=jax.ShapeDtypeStruct((team, strip_heads, head_dim + ONES, frames), F32),
        in_specs=[VMEM] * len(operands),
        out_specs=VMEM,
        scratch_shapes=[pltpu.VMEM((len(marks) * LANDMARKS, QUERY_BLOCK), BF16)] * 2,
        compiler_params=pltpu.CompilerParams(vmem_limit_bytes=16 << 20),
    )(*operands)


def far_kernel(team, sources, first, frames, head_dim, partial, *refs):
    near, far = refs[:team], refs[team:sources]
    outs = refs[sources : sources + team]
    weight_a, weight_b, scores, all_keys, all_values, held = refs[sources + team :]
    strip_heads = LANES // head_dim
    scale = head_dim**-0.5 * math.log2(math.e)
    bounds = [jnp.full((1, QUERY_BLOCK), 1.0, F32)] * 2
    heads = []

    def done(item, sums):
        n, b, h = item
        columns = pl.ds(b * QUERY_BLOCK, QUERY_BLOCK)
        sums = sums + partial[n, h, :, columns]
        total = sums[head_dim : head_dim + 1]
        bounds[:] = [jnp.minimum(bounds[0], total), jnp.maximum(bounds[1], total)]
        heads.append(sums[:head_dim] / total)
        if h == strip_heads - 1:
            outs[n][columns] = jnp.concatenate(heads, axis=0).T.astype(BF16)
            heads.clear()

    gather_sums(near, [(ref, 0) for ref in far[first:]], (weight_a, weight_b), head_dim, team, frames, done)
    unsafe = jnp.sum(jnp.where((bounds[0] > 2.0**-40) & (bounds[1] < 2.0**100), 0, 1))

    @pl.when(unsafe > 0)
    def _():
        everything = [(ref, frames) for ref in near] + [(ref, 0) for ref in far]
        for c, (ref, base) in enumerate(everything):
            all_keys[pl.ds(c * LANDMARKS, LANDMARKS)] = mark_keys_of(ref, base)
            for h in range(strip_heads):
                all_values[h * sources + c] = mark_values_of(ref, base, h, head_dim)
        lane = lax.broadcasted_iota(jnp.int32, (QUERY_BLOCK, LANES), 1)
        for n in range(team):

            def exact(i, carry):
                b, h = i // strip_heads, i % strip_heads
                block = pl.ds(pl.multiple_of(b * QUERY_BLOCK, QUERY_BLOCK), QUERY_BLOCK)
                own = (lane >= h * head_dim) & (lane < (h + 1) * head_dim)
                query = jnp.where(own, near[n][block].astype(F32), 0.0).T.astype(BF16)

                def rows_of(c):
                    return pl.ds(pl.multiple_of(c * LANDMARKS, LANDMARKS), LANDMARKS)

                def score(c, top):
                    part = dot(all_keys[rows_of(c)], query)
                    scores[rows_of(c)] = part
                    return jnp.maximum(top, jnp.max(part, axis=0, keepdims=True))

                top = lax.fori_loop(0, sources, score, jnp.full((1, QUERY_BLOCK), -jnp.inf, F32))

                def mix(c, sums):
                    weight = jnp.exp2((scores[rows_of(c)] - top) * scale).astype(BF16)
                    return sums + dot(all_values[h * sources + c], weight)

                sums = lax.fori_loop(0, sources, mix, jnp.zeros((head_dim + ONES, QUERY_BLOCK), F32))
                held[pl.ds(pl.multiple_of(h * head_dim, head_dim), head_dim)] = sums[:head_dim] / sums[head_dim : head_dim + 1]

                @pl.when(h == strip_heads - 1)
                def _():
                    outs[n][block] = held[...].T.astype(BF16)

                return carry

            lax.fori_loop(0, frames // QUERY_BLOCK * strip_heads, exact, 0)


def mix_far(partial, near, far, first, frames, head_dim):
    team, sources = len(near), len(near) + len(far)
    return pl.pallas_call(
        functools.partial(far_kernel, team, sources, first, frames, head_dim),
        out_shape=[jax.ShapeDtypeStruct((frames, LANES), BF16)] * team,
        in_specs=[VMEM] * (1 + sources),
        out_specs=[VMEM] * team,
        scratch_shapes=[
            pltpu.VMEM(((len(far) - first) * LANDMARKS, QUERY_BLOCK), BF16),
            pltpu.VMEM(((len(far) - first) * LANDMARKS, QUERY_BLOCK), BF16),
            pltpu.VMEM((sources * LANDMARKS, QUERY_BLOCK), F32),
            pltpu.VMEM((sources * LANDMARKS, LANES), BF16),
            pltpu.VMEM((LANES // head_dim * sources, head_dim + ONES, LANDMARKS), BF16),
            pltpu.VMEM((LANES, QUERY_BLOCK), F32),
        ],
        compiler_params=pltpu.CompilerParams(vmem_limit_bytes=24 << 20),
    )(partial, *near, *far)


def finish_kernel(team, streams, packs, blocks, owners, bases, offsets, w_out, gain, *refs):
    strips = refs[: team * streams]
    encoded = refs[team * streams]
    sends = refs[team * streams + 1 :]
    me = lax.axis_index("tm") % team
    my_pack = lax.axis_index("pack")
    width = streams * LANES
    model = w_out.shape[1]
    slots = packs * SLOTS * WINDOW
    owner = [owners[b, 0] for b in range(blocks)]
    starts = []
    for b in range(blocks):
        rank = jnp.int32(0)
        for a in range(b):
            rank = rank + jnp.where(owner[a] == owner[b], 1, 0)
        starts.append((jnp.bitwise_xor(owner[b], my_pack) * SLOTS + rank) * WINDOW)
    slot_row = lax.broadcasted_iota(jnp.int32, (slots, BLOCK), 0)
    slot_lane = lax.broadcasted_iota(jnp.int32, (1, slots), 1)
    hits, rows_to = [], jnp.zeros((1, slots), jnp.int32)
    for b in range(blocks):
        hits.append((slot_row == offsets[pl.ds(b, 1)] + starts[b]).astype(F32).astype(BF16))
        step = slot_lane - starts[b]
        rows_to = rows_to + jnp.where((step >= 0) & (step < WINDOW), step + (bases[0, b] + 1), 0)
    hit = jnp.concatenate(hits, axis=1)
    frame_counts = lax.dot_general(
        jnp.ones((SLOTS * WINDOW, blocks * BLOCK), BF16), hit, (((1,), (1,)), ((), ())), preferred_element_type=F32
    )
    for b in range(blocks):
        rows = pl.ds(b * BLOCK, BLOCK)
        projected = None
        for d in range(team):
            strip = jnp.concatenate([strips[s * team + d][rows] for s in range(streams)], axis=1)
            first = pl.multiple_of(jnp.bitwise_xor(me, d) * width, LANES)
            part = dot(strip, w_out[pl.ds(first, width)])
            projected = part if projected is None else projected + part
        power = jnp.mean(projected * projected, axis=-1, keepdims=True)
        encoded[rows] = (projected * lax.rsqrt(power + 1e-06) * gain[...]).astype(BF16)
    sums = dot(hit, encoded[...]).astype(BF16)
    part = SLOTS * WINDOW
    meta_row = lax.broadcasted_iota(jnp.int32, (part, slots), 0)
    meta = jnp.where(meta_row == 0, rows_to.astype(F32), jnp.where(meta_row == 1, frame_counts, 0.0))
    for e in range(packs):
        sends[e][:, pl.ds(0, model)] = sums[e * part : (e + 1) * part]
        sends[e][:, pl.ds(model, slots)] = meta.astype(BF16)


def finish(strips, w_out, gain, owners, bases, offsets, team, streams, packs):
    frames, model = strips[0].shape[0], w_out.shape[1]
    blocks = owners.shape[0]
    part = SLOTS * WINDOW
    send = jax.ShapeDtypeStruct((part, model + packs * part), BF16)
    out = pl.pallas_call(
        functools.partial(finish_kernel, team, streams, packs, blocks),
        out_shape=[jax.ShapeDtypeStruct((frames, model), BF16)] + [send] * packs,
        in_specs=[SMEM, SMEM] + [VMEM] * (3 + len(strips)),
        out_specs=[VMEM] * (1 + packs),
        compiler_params=pltpu.CompilerParams(vmem_limit_bytes=24 << 20),
        name="finish",
    )(owners, bases, offsets, w_out, gain, *strips)
    return out[0], out[1:]


def pool_kernel(packs, *refs):
    got, pooled = refs[:packs], refs[packs]
    part = SLOTS * WINDOW
    slots = packs * part
    model = pooled.shape[1]
    lane = lax.broadcasted_iota(jnp.int32, (1, slots), 1)
    rows_to, counts = jnp.zeros((1, slots), F32), jnp.zeros((1, slots), F32)
    for e in range(packs):
        meta = got[e][:, pl.ds(model, slots)].astype(F32)
        mine = (lane >= e * part) & (lane < (e + 1) * part)
        rows_to = jnp.where(mine, meta[0:1], rows_to)
        counts = jnp.where(mine, meta[1:2], counts)
    row = lax.broadcasted_iota(jnp.int32, (POOL_DEV, slots), 0)
    place = row + 1 == rows_to.astype(jnp.int32)
    total = jnp.sum(jnp.where(place, counts, 0.0), axis=1, keepdims=True)
    rows = jnp.concatenate([got[e][:, pl.ds(0, model)] for e in range(packs)], axis=0)
    sums = dot(place.astype(F32).astype(BF16), rows)
    pooled[...] = (sums / jnp.maximum(total, 1.0)).astype(BF16)


def pool(got):
    return pl.pallas_call(
        functools.partial(pool_kernel, len(got)),
        out_shape=jax.ShapeDtypeStruct((POOL_DEV, got[0].shape[1] - len(got) * SLOTS * WINDOW), BF16),
        in_specs=[VMEM] * len(got),
        out_specs=VMEM,
        compiler_params=pltpu.CompilerParams(vmem_limit_bytes=8 << 20),
        name="pool",
    )(*got)


def swap(array, axis, size, bits):
    return lax.ppermute(array, axis, [(i, i ^ bits) for i in range(size)])


def local(team, queries, keys, values, w_out, norm_gain, block_owner, block_base, frame_offset):
    q, k, v = queries[0], keys[0], values[0]
    frames, model = q.shape
    tm, packs = lax.axis_size("tm"), lax.axis_size("pack")
    head_dim = model // HEADS
    streams = model // team // LANES
    near, far, strips = [], [], []
    for s in range(streams):
        near_out, far_out = {}, {}
        for dests in marks_turns(team, s):
            outs = mark_strips(q, k, v, team, streams, s, dests, head_dim)
            near_out.update(zip(dests, outs[0]))
            far_out.update(zip(dests, outs[1]))
        far.append([swap(far_out[x % team], "tm", tm, x) for x in far_turns(team, tm)])
        near.append([near_out[0]] + [swap(near_out[d], "tm", tm, d) for d in range(1, team)])
    for s in range(streams):
        half = len(far[s]) // 2 if s == streams - 1 else 0
        partial = mix_part(near[s], near[s], frames, None, frames, head_dim)
        if half:
            partial = mix_part(near[s], far[s][:half], 0, partial, frames, head_dim)
        mixed = mix_far(partial, near[s], far[s], half, frames, head_dim)
        strips += [mixed[0]] + [swap(mixed[d], "tm", tm, d) for d in range(1, team)]
    encoded, sends = finish(
        strips, w_out, norm_gain[None], block_owner[0], block_base, frame_offset[0], team, streams, packs
    )
    got = [sends[0]] + [swap(sends[e], "pack", packs, e) for e in range(1, packs)]
    return encoded[None], pool(got)[None]


def marks_turns(team, stream):
    dests = list(reversed(range(team)))
    return [dests[: team // 2], dests[team // 2 :]] if stream == 0 else [dests]


def far_turns(team, tm):
    return [other + d for other in range(team, tm, team) for d in reversed(range(team))]


def solution(mesh):
    tm = mesh.shape["tm"]
    team = tm // 2
    return jax.shard_map(
        functools.partial(local, team),
        mesh=mesh,
        in_specs=(
            P("pack", "tm", None),
            P("pack", "tm", None),
            P("pack", "tm", None),
            P(),
            P(),
            P("pack", "tm", None),
            P("pack", "tm"),
            P("pack", "tm", None),
        ),
        out_specs=(P("pack", "tm", None), P("pack", "tm", None)),
        check_vma=False,
    )
```

```python
import functools
import math

import jax
import jax.numpy as jnp
from jax import lax
from jax.experimental import pallas as pl
from jax.experimental.pallas import tpu as pltpu
from jax.sharding import PartitionSpec as P


HEADS = 16
LANDMARKS = 256
BLOCK = 128
POOL_DEV = 128
WINDOW = 16
LANES = 128
ONES = 16
SLOTS = 2
QUERY_BLOCK = 256
BF16 = jnp.bfloat16
F32 = jnp.float32


ANY = pl.BlockSpec(memory_space=pl.ANY)
HBM = pl.BlockSpec(memory_space=pltpu.HBM)
VMEM = pl.BlockSpec(memory_space=pltpu.VMEM)
SMEM = pl.BlockSpec(memory_space=pltpu.SMEM)


def dot(a, b):
    return jnp.dot(a, b, preferred_element_type=F32)


def marks_kernel(team, streams, stream, dests, head_dim, q_hbm, k_hbm, v_hbm, *refs):
    frames = q_hbm.shape[0]
    strips = len(dests)
    near, far = refs[:strips], refs[strips : 2 * strips]
    packs, ins, score_a, score_b, in_sems, out_sems = refs[2 * strips :]
    me = lax.axis_index("tm") % team
    span = frames // LANDMARKS
    strip_heads = LANES // head_dim
    scale = head_dim**-0.5 * math.log2(math.e)
    loads = []
    for i in range(strips):
        column = pl.multiple_of((jnp.bitwise_xor(me, dests[i]) * streams + stream) * LANES, LANES)
        columns = pl.ds(column, LANES)
        three = [
            pltpu.make_async_copy(q_hbm.at[:, columns], packs.at[i, pl.ds(0, frames)], in_sems.at[i, 0]),
            pltpu.make_async_copy(k_hbm.at[:, columns], ins.at[i, 0], in_sems.at[i, 1]),
            pltpu.make_async_copy(v_hbm.at[:, columns], ins.at[i, 1], in_sems.at[i, 2]),
        ]
        for load in three:
            load.start()
        loads.append(three)
    row = lax.broadcasted_iota(jnp.int32, (LANDMARKS, frames), 0)
    frame = lax.broadcasted_iota(jnp.int32, (LANDMARKS, frames), 1)
    member = ((frame >= row * span) & (frame < (row + 1) * span)).astype(BF16)
    ones = jnp.ones((ONES, frames), BF16)
    scores = (score_a, score_b)
    stores = []

    def prepare(i):
        for load in loads[i]:
            load.wait()
        mark_q = (dot(member, packs[i, pl.ds(0, frames)]) * (1.0 / span)).astype(BF16)
        mark_k = (dot(member, ins[i, 0]) * (1.0 / span)).astype(BF16)
        packs[i, pl.ds(frames, LANDMARKS)] = mark_k
        return head_queries(mark_q, head_dim), ins[i, 1].T

    def score(i, h, slot, mark_q):
        part = dot(ins[i, 0], mark_q[h])
        scores[slot][...] = part
        return jnp.max(part, axis=0, keepdims=True)

    items = [(i, h) for i in range(strips) for h in range(strip_heads)]
    mark_q, v_next = prepare(0)
    top, heads = score(0, 0, 0, mark_q), []
    for n, (i, h) in enumerate(items):
        slot, most, v_t = n % 2, top, v_next
        if n + 1 < len(items):
            j, g = items[n + 1]
            if g == 0:
                mark_q, v_next = prepare(j)
            top = score(j, g, 1 - slot, mark_q)
        weights = jnp.exp2((scores[slot][...] - most) * scale).astype(BF16)
        mixed = dot(jnp.concatenate([v_t[h * head_dim : (h + 1) * head_dim], ones], axis=0), weights)
        heads.append(mixed[:head_dim] / mixed[head_dim : head_dim + 1])
        if h < strip_heads - 1:
            continue
        mark_v, heads = jnp.concatenate(heads, axis=0).astype(BF16), []
        for part in range(LANDMARKS // LANES):
            rows = pl.ds(frames + LANDMARKS + part * LANES, LANES)
            packs[i, rows] = mark_v[:, part * LANES : (part + 1) * LANES]
        two = [
            pltpu.make_async_copy(packs.at[i], near[i], out_sems.at[i, 0]),
            pltpu.make_async_copy(packs.at[i, pl.ds(frames, 2 * LANDMARKS)], far[i], out_sems.at[i, 1]),
        ]
        for store in two:
            store.start()
        stores += two
    for store in stores:
        store.wait()


def mark_strips(q, k, v, team, streams, stream, dests, head_dim):
    frames = q.shape[0]
    strips = len(dests)
    near = jax.ShapeDtypeStruct((frames + 2 * LANDMARKS, LANES), BF16)
    far = jax.ShapeDtypeStruct((2 * LANDMARKS, LANES), BF16)
    out = pl.pallas_call(
        functools.partial(marks_kernel, team, streams, stream, dests, head_dim),
        out_shape=[near] * strips + [far] * strips,
        in_specs=[HBM] * 3,
        out_specs=[ANY] * (2 * strips),
        scratch_shapes=[
            pltpu.VMEM((strips, frames + 2 * LANDMARKS, LANES), BF16),
            pltpu.VMEM((strips, 2, frames, LANES), BF16),
            pltpu.VMEM((frames, LANDMARKS), F32),
            pltpu.VMEM((frames, LANDMARKS), F32),
            pltpu.SemaphoreType.DMA((strips, 3)),
            pltpu.SemaphoreType.DMA((strips, 2)),
        ],
        compiler_params=pltpu.CompilerParams(vmem_limit_bytes=60 << 20),
    )(q, k, v)
    return out[:strips], out[strips:]


def head_queries(block, head_dim):
    flat = block.T
    parts = []
    for low in range(0, LANES, head_dim):
        pieces = [jnp.zeros((low, flat.shape[1]), BF16), flat[low : low + head_dim]]
        pieces.append(jnp.zeros((LANES - low - head_dim, flat.shape[1]), BF16))
        parts.append(jnp.concatenate([piece for piece in pieces if piece.shape[0]], axis=0))
    return parts


def mark_keys_of(ref, base):
    return ref[pl.ds(base, LANDMARKS)]


def mark_values_of(ref, base, h, head_dim):
    parts = [
        ref[pl.ds(base + LANDMARKS + part * LANES + h * head_dim, head_dim)] for part in range(LANDMARKS // LANES)
    ]
    return jnp.concatenate([jnp.concatenate(parts, axis=1), jnp.ones((ONES, LANDMARKS), BF16)], axis=0)


def query_items(frames, head_dim, dests):
    return [(n, b, h) for n in range(dests) for b in range(frames // QUERY_BLOCK) for h in range(LANES // head_dim)]


def gather_sums(queries, sources, weights, head_dim, dests, frames, done):
    scale = head_dim**-0.5 * math.log2(math.e)
    items = query_items(frames, head_dim, dests)
    for i in range(len(items) + 1):
        if i < len(items):
            n, b, h = items[i]
            if h == 0:
                heads = head_queries(queries[n][pl.ds(b * QUERY_BLOCK, QUERY_BLOCK)], head_dim)
            query = heads[h]
        for c, (ref, base) in enumerate(sources):
            rows = pl.ds(c * LANDMARKS, LANDMARKS)
            if i < len(items):
                weights[i % 2][rows] = jnp.exp2(dot(mark_keys_of(ref, base), query) * scale).astype(BF16)
            if i > 0:
                part = dot(mark_values_of(ref, base, items[i - 1][2], head_dim), weights[1 - i % 2][rows])
                sums = part if c == 0 else sums + part
        if i > 0:
            done(items[i - 1], sums)


def part_kernel(team, sources, base, frames, head_dim, more, *refs):
    queries, marks = refs[:team], refs[team : team + sources]
    before, refs = (refs[team + sources], refs[team + sources + 1 :]) if more else (None, refs[team + sources :])
    partial, weights = refs[0], refs[1:]

    def done(item, sums):
        n, b, h = item
        columns = pl.ds(b * QUERY_BLOCK, QUERY_BLOCK)
        partial[n, h, :, columns] = sums + before[n, h, :, columns] if more else sums

    gather_sums(queries, [(ref, base) for ref in marks], weights, head_dim, team, frames, done)


def mix_part(near, marks, base, before, frames, head_dim):
    team, strip_heads = len(near), LANES // head_dim
    more = before is not None
    operands = [*near, *marks] + ([before] if more else [])
    return pl.pallas_call(
        functools.partial(part_kernel, team, len(marks), base, frames, head_dim, more),
        out_shape=jax.ShapeDtypeStruct((team, strip_heads, head_dim + ONES, frames), F32),
        in_specs=[VMEM] * len(operands),
        out_specs=VMEM,
        scratch_shapes=[pltpu.VMEM((len(marks) * LANDMARKS, QUERY_BLOCK), BF16)] * 2,
        compiler_params=pltpu.CompilerParams(vmem_limit_bytes=16 << 20),
    )(*operands)


def far_kernel(team, sources, first, frames, head_dim, partial, *refs):
    near, far = refs[:team], refs[team:sources]
    outs = refs[sources : sources + team]
    weight_a, weight_b, scores, all_keys, all_values, held = refs[sources + team :]
    strip_heads = LANES // head_dim
    scale = head_dim**-0.5 * math.log2(math.e)
    bounds = [jnp.full((1, QUERY_BLOCK), 1.0, F32)] * 2
    heads = []

    def done(item, sums):
        n, b, h = item
        columns = pl.ds(b * QUERY_BLOCK, QUERY_BLOCK)
        sums = sums + partial[n, h, :, columns]
        total = sums[head_dim : head_dim + 1]
        bounds[:] = [jnp.minimum(bounds[0], total), jnp.maximum(bounds[1], total)]
        heads.append(sums[:head_dim] / total)
        if h == strip_heads - 1:
            outs[n][columns] = jnp.concatenate(heads, axis=0).T.astype(BF16)
            heads.clear()

    gather_sums(near, [(ref, 0) for ref in far[first:]], (weight_a, weight_b), head_dim, team, frames, done)
    unsafe = jnp.sum(jnp.where((bounds[0] > 2.0**-40) & (bounds[1] < 2.0**100), 0, 1))

    @pl.when(unsafe > 0)
    def _():
        everything = [(ref, frames) for ref in near] + [(ref, 0) for ref in far]
        for c, (ref, base) in enumerate(everything):
            all_keys[pl.ds(c * LANDMARKS, LANDMARKS)] = mark_keys_of(ref, base)
            for h in range(strip_heads):
                all_values[h * sources + c] = mark_values_of(ref, base, h, head_dim)
        lane = lax.broadcasted_iota(jnp.int32, (QUERY_BLOCK, LANES), 1)
        for n in range(team):

            def exact(i, carry):
                b, h = i // strip_heads, i % strip_heads
                block = pl.ds(pl.multiple_of(b * QUERY_BLOCK, QUERY_BLOCK), QUERY_BLOCK)
                own = (lane >= h * head_dim) & (lane < (h + 1) * head_dim)
                query = jnp.where(own, near[n][block].astype(F32), 0.0).T.astype(BF16)

                def rows_of(c):
                    return pl.ds(pl.multiple_of(c * LANDMARKS, LANDMARKS), LANDMARKS)

                def score(c, top):
                    part = dot(all_keys[rows_of(c)], query)
                    scores[rows_of(c)] = part
                    return jnp.maximum(top, jnp.max(part, axis=0, keepdims=True))

                top = lax.fori_loop(0, sources, score, jnp.full((1, QUERY_BLOCK), -jnp.inf, F32))

                def mix(c, sums):
                    weight = jnp.exp2((scores[rows_of(c)] - top) * scale).astype(BF16)
                    return sums + dot(all_values[h * sources + c], weight)

                sums = lax.fori_loop(0, sources, mix, jnp.zeros((head_dim + ONES, QUERY_BLOCK), F32))
                held[pl.ds(pl.multiple_of(h * head_dim, head_dim), head_dim)] = sums[:head_dim] / sums[head_dim : head_dim + 1]

                @pl.when(h == strip_heads - 1)
                def _():
                    outs[n][block] = held[...].T.astype(BF16)

                return carry

            lax.fori_loop(0, frames // QUERY_BLOCK * strip_heads, exact, 0)


def mix_far(partial, near, far, first, frames, head_dim):
    team, sources = len(near), len(near) + len(far)
    return pl.pallas_call(
        functools.partial(far_kernel, team, sources, first, frames, head_dim),
        out_shape=[jax.ShapeDtypeStruct((frames, LANES), BF16)] * team,
        in_specs=[VMEM] * (1 + sources),
        out_specs=[VMEM] * team,
        scratch_shapes=[
            pltpu.VMEM(((len(far) - first) * LANDMARKS, QUERY_BLOCK), BF16),
            pltpu.VMEM(((len(far) - first) * LANDMARKS, QUERY_BLOCK), BF16),
            pltpu.VMEM((sources * LANDMARKS, QUERY_BLOCK), F32),
            pltpu.VMEM((sources * LANDMARKS, LANES), BF16),
            pltpu.VMEM((LANES // head_dim * sources, head_dim + ONES, LANDMARKS), BF16),
            pltpu.VMEM((LANES, QUERY_BLOCK), F32),
        ],
        compiler_params=pltpu.CompilerParams(vmem_limit_bytes=24 << 20),
    )(partial, *near, *far)


def finish_kernel(team, streams, packs, blocks, owners, bases, offsets, w_out, gain, *refs):
    strips = refs[: team * streams]
    encoded = refs[team * streams]
    sends = refs[team * streams + 1 :]
    me = lax.axis_index("tm") % team
    my_pack = lax.axis_index("pack")
    width = streams * LANES
    model = w_out.shape[1]
    slots = packs * SLOTS * WINDOW
    owner = [owners[b, 0] for b in range(blocks)]
    starts = []
    for b in range(blocks):
        rank = jnp.int32(0)
        for a in range(b):
            rank = rank + jnp.where(owner[a] == owner[b], 1, 0)
        starts.append((jnp.bitwise_xor(owner[b], my_pack) * SLOTS + rank) * WINDOW)
    slot_row = lax.broadcasted_iota(jnp.int32, (slots, BLOCK), 0)
    slot_lane = lax.broadcasted_iota(jnp.int32, (1, slots), 1)
    hits, rows_to = [], jnp.zeros((1, slots), jnp.int32)
    for b in range(blocks):
        hits.append((slot_row == offsets[pl.ds(b, 1)] + starts[b]).astype(F32).astype(BF16))
        step = slot_lane - starts[b]
        rows_to = rows_to + jnp.where((step >= 0) & (step < WINDOW), step + (bases[0, b] + 1), 0)
    hit = jnp.concatenate(hits, axis=1)
    frame_counts = lax.dot_general(
        jnp.ones((SLOTS * WINDOW, blocks * BLOCK), BF16), hit, (((1,), (1,)), ((), ())), preferred_element_type=F32
    )
    for b in range(blocks):
        rows = pl.ds(b * BLOCK, BLOCK)
        projected = None
        for d in range(team):
            strip = jnp.concatenate([strips[s * team + d][rows] for s in range(streams)], axis=1)
            first = pl.multiple_of(jnp.bitwise_xor(me, d) * width, LANES)
            part = dot(strip, w_out[pl.ds(first, width)])
            projected = part if projected is None else projected + part
        power = jnp.mean(projected * projected, axis=-1, keepdims=True)
        encoded[rows] = (projected * lax.rsqrt(power + 1e-06) * gain[...]).astype(BF16)
    sums = dot(hit, encoded[...]).astype(BF16)
    part = SLOTS * WINDOW
    meta_row = lax.broadcasted_iota(jnp.int32, (part, slots), 0)
    meta = jnp.where(meta_row == 0, rows_to.astype(F32), jnp.where(meta_row == 1, frame_counts, 0.0))
    for e in range(packs):
        sends[e][:, pl.ds(0, model)] = sums[e * part : (e + 1) * part]
        sends[e][:, pl.ds(model, slots)] = meta.astype(BF16)


def finish(strips, w_out, gain, owners, bases, offsets, team, streams, packs):
    frames, model = strips[0].shape[0], w_out.shape[1]
    blocks = owners.shape[0]
    part = SLOTS * WINDOW
    send = jax.ShapeDtypeStruct((part, model + packs * part), BF16)
    out = pl.pallas_call(
        functools.partial(finish_kernel, team, streams, packs, blocks),
        out_shape=[jax.ShapeDtypeStruct((frames, model), BF16)] + [send] * packs,
        in_specs=[SMEM, SMEM] + [VMEM] * (3 + len(strips)),
        out_specs=[VMEM] * (1 + packs),
        compiler_params=pltpu.CompilerParams(vmem_limit_bytes=24 << 20),
        name="finish",
    )(owners, bases, offsets, w_out, gain, *strips)
    return out[0], out[1:]


def pool_kernel(packs, *refs):
    got, pooled = refs[:packs], refs[packs]
    part = SLOTS * WINDOW
    slots = packs * part
    model = pooled.shape[1]
    lane = lax.broadcasted_iota(jnp.int32, (1, slots), 1)
    rows_to, counts = jnp.zeros((1, slots), F32), jnp.zeros((1, slots), F32)
    for e in range(packs):
        meta = got[e][:, pl.ds(model, slots)].astype(F32)
        mine = (lane >= e * part) & (lane < (e + 1) * part)
        rows_to = jnp.where(mine, meta[0:1], rows_to)
        counts = jnp.where(mine, meta[1:2], counts)
    row = lax.broadcasted_iota(jnp.int32, (POOL_DEV, slots), 0)
    place = row + 1 == rows_to.astype(jnp.int32)
    total = jnp.sum(jnp.where(place, counts, 0.0), axis=1, keepdims=True)
    rows = jnp.concatenate([got[e][:, pl.ds(0, model)] for e in range(packs)], axis=0)
    sums = dot(place.astype(F32).astype(BF16), rows)
    pooled[...] = (sums / jnp.maximum(total, 1.0)).astype(BF16)


def pool(got):
    return pl.pallas_call(
        functools.partial(pool_kernel, len(got)),
        out_shape=jax.ShapeDtypeStruct((POOL_DEV, got[0].shape[1] - len(got) * SLOTS * WINDOW), BF16),
        in_specs=[VMEM] * len(got),
        out_specs=VMEM,
        compiler_params=pltpu.CompilerParams(vmem_limit_bytes=8 << 20),
        name="pool",
    )(*got)


def swap(array, axis, size, bits):
    return lax.ppermute(array, axis, [(i, i ^ bits) for i in range(size)])


def local(team, queries, keys, values, w_out, norm_gain, block_owner, block_base, frame_offset):
    q, k, v = queries[0], keys[0], values[0]
    frames, model = q.shape
    tm, packs = lax.axis_size("tm"), lax.axis_size("pack")
    head_dim = model // HEADS
    streams = model // team // LANES
    near, far, strips = [], [], []
    for s in range(streams):
        near_out, far_out = {}, {}
        for dests in marks_turns(team, s):
            outs = mark_strips(q, k, v, team, streams, s, dests, head_dim)
            near_out.update(zip(dests, outs[0]))
            far_out.update(zip(dests, outs[1]))
        far.append([swap(far_out[x % team], "tm", tm, x) for x in far_turns(team, tm)])
        near.append([near_out[0]] + [swap(near_out[d], "tm", tm, d) for d in range(1, team)])
    for s in range(streams):
        half = len(far[s]) // 2 if s == streams - 1 else 0
        partial = mix_part(near[s], near[s], frames, None, frames, head_dim)
        if half:
            partial = mix_part(near[s], far[s][:half], 0, partial, frames, head_dim)
        mixed = mix_far(partial, near[s], far[s], half, frames, head_dim)
        strips += [mixed[0]] + [swap(mixed[d], "tm", tm, d) for d in range(1, team)]
    encoded, sends = finish(
        strips, w_out, norm_gain[None], block_owner[0], block_base, frame_offset[0], team, streams, packs
    )
    got = [sends[0]] + [swap(sends[e], "pack", packs, e) for e in range(1, packs)]
    return encoded[None], pool(got)[None]


def marks_turns(team, stream):
    dests = list(reversed(range(team)))
    return [dests[: team // 2], dests[team // 2 :]] if stream == 0 else [dests]


def far_turns(team, tm):
    return [other + d for other in range(team, tm, team) for d in reversed(range(team))]


def solution(mesh):
    tm = mesh.shape["tm"]
    team = tm // 2
    return jax.shard_map(
        functools.partial(local, team),
        mesh=mesh,
        in_specs=(
            P("pack", "tm", None),
            P("pack", "tm", None),
            P("pack", "tm", None),
            P(),
            P(),
            P("pack", "tm", None),
            P("pack", "tm"),
            P("pack", "tm", None),
        ),
        out_specs=(P("pack", "tm", None), P("pack", "tm", None)),
        check_vma=False,
    )
```

```python
import functools
import math

import jax
import jax.numpy as jnp
from jax import lax
from jax.experimental import pallas as pl
from jax.experimental.pallas import tpu as pltpu
from jax.sharding import PartitionSpec as P


HEADS = 16
LANDMARKS = 256
BLOCK = 128
POOL_DEV = 128
WINDOW = 16
LANES = 128
ONES = 16
SLOTS = 2
QUERY_BLOCK = 512
BF16 = jnp.bfloat16
F32 = jnp.float32


ANY = pl.BlockSpec(memory_space=pl.ANY)
HBM = pl.BlockSpec(memory_space=pltpu.HBM)
VMEM = pl.BlockSpec(memory_space=pltpu.VMEM)
SMEM = pl.BlockSpec(memory_space=pltpu.SMEM)


def dot(a, b):
    return jnp.dot(a, b, preferred_element_type=F32)


def marks_kernel(team, streams, stream, dests, head_dim, q_hbm, k_hbm, v_hbm, *refs):
    frames = q_hbm.shape[0]
    strips = len(dests)
    near, far = refs[:strips], refs[strips : 2 * strips]
    packs, ins, score_a, score_b, in_sems, out_sems = refs[2 * strips :]
    me = lax.axis_index("tm") % team
    span = frames // LANDMARKS
    strip_heads = LANES // head_dim
    scale = head_dim**-0.5 * math.log2(math.e)
    loads = []
    for i in range(strips):
        column = pl.multiple_of((jnp.bitwise_xor(me, dests[i]) * streams + stream) * LANES, LANES)
        columns = pl.ds(column, LANES)
        three = [
            pltpu.make_async_copy(q_hbm.at[:, columns], packs.at[i, pl.ds(0, frames)], in_sems.at[i, 0]),
            pltpu.make_async_copy(k_hbm.at[:, columns], ins.at[i, 0], in_sems.at[i, 1]),
            pltpu.make_async_copy(v_hbm.at[:, columns], ins.at[i, 1], in_sems.at[i, 2]),
        ]
        for load in three:
            load.start()
        loads.append(three)
    row = lax.broadcasted_iota(jnp.int32, (LANDMARKS, frames), 0)
    frame = lax.broadcasted_iota(jnp.int32, (LANDMARKS, frames), 1)
    member = ((frame >= row * span) & (frame < (row + 1) * span)).astype(BF16)
    ones = jnp.ones((ONES, frames), BF16)
    scores = (score_a, score_b)
    stores = []

    def prepare(i):
        for load in loads[i]:
            load.wait()
        mark_q = (dot(member, packs[i, pl.ds(0, frames)]) * (1.0 / span)).astype(BF16)
        mark_k = (dot(member, ins[i, 0]) * (1.0 / span)).astype(BF16)
        packs[i, pl.ds(frames, LANDMARKS)] = mark_k
        return head_queries(mark_q, head_dim), ins[i, 1].T

    def score(i, h, slot, mark_q):
        part = dot(ins[i, 0], mark_q[h])
        scores[slot][...] = part
        return jnp.max(part, axis=0, keepdims=True)

    items = [(i, h) for i in range(strips) for h in range(strip_heads)]
    mark_q, v_next = prepare(0)
    top, heads = score(0, 0, 0, mark_q), []
    for n, (i, h) in enumerate(items):
        slot, most, v_t = n % 2, top, v_next
        if n + 1 < len(items):
            j, g = items[n + 1]
            if g == 0:
                mark_q, v_next = prepare(j)
            top = score(j, g, 1 - slot, mark_q)
        weights = jnp.exp2((scores[slot][...] - most) * scale).astype(BF16)
        mixed = dot(jnp.concatenate([v_t[h * head_dim : (h + 1) * head_dim], ones], axis=0), weights)
        heads.append(mixed[:head_dim] * (1.0 / mixed[head_dim : head_dim + 1]))
        if h < strip_heads - 1:
            continue
        mark_v, heads = jnp.concatenate(heads, axis=0).astype(BF16), []
        for part in range(LANDMARKS // LANES):
            rows = pl.ds(frames + LANDMARKS + part * LANES, LANES)
            packs[i, rows] = mark_v[:, part * LANES : (part + 1) * LANES]
        two = [
            pltpu.make_async_copy(packs.at[i], near[i], out_sems.at[i, 0]),
            pltpu.make_async_copy(packs.at[i, pl.ds(frames, 2 * LANDMARKS)], far[i], out_sems.at[i, 1]),
        ]
        for store in two:
            store.start()
        stores += two
    for store in stores:
        store.wait()


def mark_strips(q, k, v, team, streams, stream, dests, head_dim):
    frames = q.shape[0]
    strips = len(dests)
    near = jax.ShapeDtypeStruct((frames + 2 * LANDMARKS, LANES), BF16)
    far = jax.ShapeDtypeStruct((2 * LANDMARKS, LANES), BF16)
    out = pl.pallas_call(
        functools.partial(marks_kernel, team, streams, stream, dests, head_dim),
        out_shape=[near] * strips + [far] * strips,
        in_specs=[HBM] * 3,
        out_specs=[ANY] * (2 * strips),
        scratch_shapes=[
            pltpu.VMEM((strips, frames + 2 * LANDMARKS, LANES), BF16),
            pltpu.VMEM((strips, 2, frames, LANES), BF16),
            pltpu.VMEM((frames, LANDMARKS), F32),
            pltpu.VMEM((frames, LANDMARKS), F32),
            pltpu.SemaphoreType.DMA((strips, 3)),
            pltpu.SemaphoreType.DMA((strips, 2)),
        ],
        compiler_params=pltpu.CompilerParams(vmem_limit_bytes=60 << 20),
    )(q, k, v)
    return out[:strips], out[strips:]


def head_queries(block, head_dim):
    flat = block.T
    parts = []
    for low in range(0, LANES, head_dim):
        pieces = [jnp.zeros((low, flat.shape[1]), BF16), flat[low : low + head_dim]]
        pieces.append(jnp.zeros((LANES - low - head_dim, flat.shape[1]), BF16))
        parts.append(jnp.concatenate([piece for piece in pieces if piece.shape[0]], axis=0))
    return parts


def mark_keys_of(ref, base):
    return ref[pl.ds(base, LANDMARKS)]


def mark_values_of(ref, base, h, head_dim):
    parts = [
        ref[pl.ds(base + LANDMARKS + part * LANES + h * head_dim, head_dim)] for part in range(LANDMARKS // LANES)
    ]
    return jnp.concatenate([jnp.concatenate(parts, axis=1), jnp.ones((ONES, LANDMARKS), BF16)], axis=0)


def query_items(frames, head_dim, dests):
    return [(n, b, h) for n in range(dests) for b in range(frames // QUERY_BLOCK) for h in range(LANES // head_dim)]


def gather_sums(queries, sources, weights, head_dim, dests, frames, done):
    scale = head_dim**-0.5 * math.log2(math.e)
    items = query_items(frames, head_dim, dests)
    for i in range(len(items) + 1):
        if i < len(items):
            n, b, h = items[i]
            if h == 0:
                heads = head_queries(queries[n][pl.ds(b * QUERY_BLOCK, QUERY_BLOCK)], head_dim)
            query = heads[h]
        for c, (ref, base) in enumerate(sources):
            rows = pl.ds(c * LANDMARKS, LANDMARKS)
            if i < len(items):
                weights[i % 2][rows] = jnp.exp2(dot(mark_keys_of(ref, base), query) * scale).astype(BF16)
            if i > 0:
                part = dot(mark_values_of(ref, base, items[i - 1][2], head_dim), weights[1 - i % 2][rows])
                sums = part if c == 0 else sums + part
        if i > 0:
            done(items[i - 1], sums)


def part_kernel(team, sources, base, frames, head_dim, more, *refs):
    queries, marks = refs[:team], refs[team : team + sources]
    before, refs = (refs[team + sources], refs[team + sources + 1 :]) if more else (None, refs[team + sources :])
    partial, weights = refs[0], refs[1:]

    def done(item, sums):
        n, b, h = item
        columns = pl.ds(b * QUERY_BLOCK, QUERY_BLOCK)
        partial[n, h, :, columns] = sums + before[n, h, :, columns] if more else sums

    gather_sums(queries, [(ref, base) for ref in marks], weights, head_dim, team, frames, done)


def mix_part(near, marks, base, before, frames, head_dim):
    team, strip_heads = len(near), LANES // head_dim
    more = before is not None
    operands = [*near, *marks] + ([before] if more else [])
    return pl.pallas_call(
        functools.partial(part_kernel, team, len(marks), base, frames, head_dim, more),
        out_shape=jax.ShapeDtypeStruct((team, strip_heads, head_dim + ONES, frames), F32),
        in_specs=[VMEM] * len(operands),
        out_specs=VMEM,
        scratch_shapes=[pltpu.VMEM((len(marks) * LANDMARKS, QUERY_BLOCK), BF16)] * 2,
        compiler_params=pltpu.CompilerParams(vmem_limit_bytes=16 << 20),
    )(*operands)


def far_kernel(team, sources, first, frames, head_dim, partial, *refs):
    near, far = refs[:team], refs[team:sources]
    outs = refs[sources : sources + team]
    weight_a, weight_b, scores, all_keys, all_values, held = refs[sources + team :]
    strip_heads = LANES // head_dim
    scale = head_dim**-0.5 * math.log2(math.e)
    bounds = [jnp.full((1, QUERY_BLOCK), 1.0, F32)] * 2
    heads = []

    def done(item, sums):
        n, b, h = item
        columns = pl.ds(b * QUERY_BLOCK, QUERY_BLOCK)
        sums = sums + partial[n, h, :, columns]
        total = sums[head_dim : head_dim + 1]
        bounds[:] = [jnp.minimum(bounds[0], total), jnp.maximum(bounds[1], total)]
        heads.append((sums[:head_dim] * (1.0 / total)).astype(BF16))
        if h == strip_heads - 1:
            outs[n][columns] = jnp.concatenate(heads, axis=0).T
            heads.clear()

    gather_sums(near, [(ref, 0) for ref in far[first:]], (weight_a, weight_b), head_dim, team, frames, done)
    unsafe = jnp.sum(jnp.where((bounds[0] > 2.0**-40) & (bounds[1] < 2.0**100), 0, 1))

    @pl.when(unsafe > 0)
    def _():
        everything = [(ref, frames) for ref in near] + [(ref, 0) for ref in far]
        for c, (ref, base) in enumerate(everything):
            all_keys[pl.ds(c * LANDMARKS, LANDMARKS)] = mark_keys_of(ref, base)
            for h in range(strip_heads):
                all_values[h * sources + c] = mark_values_of(ref, base, h, head_dim)
        lane = lax.broadcasted_iota(jnp.int32, (QUERY_BLOCK, LANES), 1)
        for n in range(team):

            def exact(i, carry):
                b, h = i // strip_heads, i % strip_heads
                block = pl.ds(pl.multiple_of(b * QUERY_BLOCK, QUERY_BLOCK), QUERY_BLOCK)
                own = (lane >= h * head_dim) & (lane < (h + 1) * head_dim)
                query = jnp.where(own, near[n][block].astype(F32), 0.0).T.astype(BF16)

                def rows_of(c):
                    return pl.ds(pl.multiple_of(c * LANDMARKS, LANDMARKS), LANDMARKS)

                def score(c, top):
                    part = dot(all_keys[rows_of(c)], query)
                    scores[rows_of(c)] = part
                    return jnp.maximum(top, jnp.max(part, axis=0, keepdims=True))

                top = lax.fori_loop(0, sources, score, jnp.full((1, QUERY_BLOCK), -jnp.inf, F32))

                def mix(c, sums):
                    weight = jnp.exp2((scores[rows_of(c)] - top) * scale).astype(BF16)
                    return sums + dot(all_values[h * sources + c], weight)

                sums = lax.fori_loop(0, sources, mix, jnp.zeros((head_dim + ONES, QUERY_BLOCK), F32))
                held[pl.ds(pl.multiple_of(h * head_dim, head_dim), head_dim)] = sums[:head_dim] / sums[head_dim : head_dim + 1]

                @pl.when(h == strip_heads - 1)
                def _():
                    outs[n][block] = held[...].T.astype(BF16)

                return carry

            lax.fori_loop(0, frames // QUERY_BLOCK * strip_heads, exact, 0)


def mix_far(partial, near, far, first, frames, head_dim):
    team, sources = len(near), len(near) + len(far)
    return pl.pallas_call(
        functools.partial(far_kernel, team, sources, first, frames, head_dim),
        out_shape=[jax.ShapeDtypeStruct((frames, LANES), BF16)] * team,
        in_specs=[VMEM] * (1 + sources),
        out_specs=[VMEM] * team,
        scratch_shapes=[
            pltpu.VMEM(((len(far) - first) * LANDMARKS, QUERY_BLOCK), BF16),
            pltpu.VMEM(((len(far) - first) * LANDMARKS, QUERY_BLOCK), BF16),
            pltpu.VMEM((sources * LANDMARKS, QUERY_BLOCK), F32),
            pltpu.VMEM((sources * LANDMARKS, LANES), BF16),
            pltpu.VMEM((LANES // head_dim * sources, head_dim + ONES, LANDMARKS), BF16),
            pltpu.VMEM((LANES, QUERY_BLOCK), F32),
        ],
        compiler_params=pltpu.CompilerParams(vmem_limit_bytes=24 << 20),
    )(partial, *near, *far)


def strips_product(strips, places, rows, w_out, me, streams):
    total = None
    for i in range(0, len(strips), 2):
        left, right = [], []
        for strip, (s, d) in zip(strips[i : i + 2], places[i : i + 2]):
            first = pl.multiple_of((jnp.bitwise_xor(me, d) * streams + s) * LANES, LANES)
            left.append(strip[rows])
            right.append(w_out[pl.ds(first, LANES)])
        part = dot(jnp.concatenate(left, axis=1), jnp.concatenate(right, axis=0))
        total = part if total is None else total + part
    return total


def project_kernel(team, streams, places, w_out, *refs):
    strips, projected = refs[:-1], refs[-1]
    me = lax.axis_index("tm") % team
    for b in range(projected.shape[0] // BLOCK):
        rows = pl.ds(b * BLOCK, BLOCK)
        projected[rows] = strips_product(strips, places, rows, w_out, me, streams)


def project(strips, places, w_out, team, streams):
    return pl.pallas_call(
        functools.partial(project_kernel, team, streams, places),
        out_shape=jax.ShapeDtypeStruct((strips[0].shape[0], w_out.shape[1]), F32),
        in_specs=[VMEM] * (1 + len(strips)),
        out_specs=VMEM,
        compiler_params=pltpu.CompilerParams(vmem_limit_bytes=16 << 20),
        name="project",
    )(w_out, *strips)


def finish_kernel(team, streams, packs, blocks, places, owners, bases, offsets, w_out, gain, begun, *refs):
    strips, refs = refs[: len(places)], refs[len(places) :]
    encoded_out, sends, (encoded, sems) = refs[0], refs[1 : 1 + packs], refs[1 + packs :]
    me = lax.axis_index("tm") % team
    my_pack = lax.axis_index("pack")
    model = w_out.shape[1]
    slots = packs * SLOTS * WINDOW
    owner = [owners[b, 0] for b in range(blocks)]
    starts = []
    for b in range(blocks):
        rank = jnp.int32(0)
        for a in range(b):
            rank = rank + jnp.where(owner[a] == owner[b], 1, 0)
        starts.append((jnp.bitwise_xor(owner[b], my_pack) * SLOTS + rank) * WINDOW)
    slot_row = lax.broadcasted_iota(jnp.int32, (slots, BLOCK), 0)
    slot_lane = lax.broadcasted_iota(jnp.int32, (1, slots), 1)
    hits, rows_to = [], jnp.zeros((1, slots), jnp.int32)
    for b in range(blocks):
        hits.append((slot_row == offsets[pl.ds(b, 1)] + starts[b]).astype(F32).astype(BF16))
        step = slot_lane - starts[b]
        rows_to = rows_to + jnp.where((step >= 0) & (step < WINDOW), step + (bases[0, b] + 1), 0)
    hit = jnp.concatenate(hits, axis=1)
    frame_counts = lax.dot_general(
        jnp.ones((SLOTS * WINDOW, blocks * BLOCK), BF16), hit, (((1,), (1,)), ((), ())), preferred_element_type=F32
    )
    copies = []
    for b in range(blocks):
        rows = pl.ds(b * BLOCK, BLOCK)
        projected = begun[rows] + strips_product(strips, places, rows, w_out, me, streams)
        power = jnp.mean(projected * projected, axis=-1, keepdims=True)
        encoded[rows] = (projected * lax.rsqrt(power + 1e-06) * gain[...]).astype(BF16)
        copies.append(pltpu.make_async_copy(encoded.at[rows], encoded_out.at[rows], sems.at[b]))
        copies[-1].start()
    sums = dot(hit, encoded[...]).astype(BF16)
    part = SLOTS * WINDOW
    meta_row = lax.broadcasted_iota(jnp.int32, (part, slots), 0)
    meta = jnp.where(meta_row == 0, rows_to.astype(F32), jnp.where(meta_row == 1, frame_counts, 0.0))
    for e in range(packs):
        sends[e][:, pl.ds(0, model)] = sums[e * part : (e + 1) * part]
        sends[e][:, pl.ds(model, slots)] = meta.astype(BF16)
    for copy in copies:
        copy.wait()


def finish(begun, strips, places, w_out, gain, owners, bases, offsets, team, streams, packs):
    frames, model = begun.shape
    blocks = owners.shape[0]
    part = SLOTS * WINDOW
    send = jax.ShapeDtypeStruct((part, model + packs * part), BF16)
    out = pl.pallas_call(
        functools.partial(finish_kernel, team, streams, packs, blocks, places),
        out_shape=[jax.ShapeDtypeStruct((frames, model), BF16)] + [send] * packs,
        in_specs=[SMEM, SMEM] + [VMEM] * (4 + len(strips)),
        out_specs=[ANY] + [VMEM] * packs,
        scratch_shapes=[pltpu.VMEM((frames, model), BF16), pltpu.SemaphoreType.DMA((blocks,))],
        compiler_params=pltpu.CompilerParams(vmem_limit_bytes=16 << 20),
        name="finish",
    )(owners, bases, offsets, w_out, gain, begun, *strips)
    return out[0], out[1:]


def pool_kernel(packs, *refs):
    got, pooled = refs[:packs], refs[packs]
    part = SLOTS * WINDOW
    slots = packs * part
    model = pooled.shape[1]
    lane = lax.broadcasted_iota(jnp.int32, (1, slots), 1)
    rows_to, counts = jnp.zeros((1, slots), F32), jnp.zeros((1, slots), F32)
    for e in range(packs):
        meta = got[e][:, pl.ds(model, slots)].astype(F32)
        mine = (lane >= e * part) & (lane < (e + 1) * part)
        rows_to = jnp.where(mine, meta[0:1], rows_to)
        counts = jnp.where(mine, meta[1:2], counts)
    row = lax.broadcasted_iota(jnp.int32, (POOL_DEV, slots), 0)
    place = row + 1 == rows_to.astype(jnp.int32)
    total = jnp.sum(jnp.where(place, counts, 0.0), axis=1, keepdims=True)
    rows = jnp.concatenate([got[e][:, pl.ds(0, model)] for e in range(packs)], axis=0)
    sums = dot(place.astype(F32).astype(BF16), rows)
    pooled[...] = (sums / jnp.maximum(total, 1.0)).astype(BF16)


def pool(got):
    return pl.pallas_call(
        functools.partial(pool_kernel, len(got)),
        out_shape=jax.ShapeDtypeStruct((POOL_DEV, got[0].shape[1] - len(got) * SLOTS * WINDOW), BF16),
        in_specs=[VMEM] * len(got),
        out_specs=VMEM,
        compiler_params=pltpu.CompilerParams(vmem_limit_bytes=8 << 20),
        name="pool",
    )(*got)


def swap(array, axis, size, bits):
    return lax.ppermute(array, axis, [(i, i ^ bits) for i in range(size)])


def local(team, queries, keys, values, w_out, norm_gain, block_owner, block_base, frame_offset):
    q, k, v = queries[0], keys[0], values[0]
    frames, model = q.shape
    tm, packs = lax.axis_size("tm"), lax.axis_size("pack")
    head_dim = model // HEADS
    streams = model // team // LANES
    near, far, strips = [], [], {}
    for s in range(streams):
        near_out, far_out = {}, {}
        for dests in marks_turns(team, s):
            outs = mark_strips(q, k, v, team, streams, s, dests, head_dim)
            near_out.update(zip(dests, outs[0]))
            far_out.update(zip(dests, outs[1]))
        far.append([swap(far_out[x % team], "tm", tm, x) for x in far_turns(team, tm)])
        near.append([near_out[0]] + [swap(near_out[d], "tm", tm, d) for d in range(1, team)])
    for s in range(streams):
        half = len(far[s]) // 2 if s == streams - 1 else 0
        partial = mix_part(near[s], near[s], frames, None, frames, head_dim)
        if half:
            partial = mix_part(near[s], far[s][:half], 0, partial, frames, head_dim)
        mixed = mix_far(partial, near[s], far[s], half, frames, head_dim)
        strips[s, 0] = mixed[0]
        strips.update({(s, d): swap(mixed[d], "tm", tm, d) for d in range(1, team)})
    ends = [(streams - 1, d) for d in range(1, team)]
    early = [place for place in strips if place not in ends]
    begun = project([strips[place] for place in early], early, w_out, team, streams)
    encoded, sends = finish(
        begun,
        [strips[place] for place in ends],
        ends,
        w_out,
        norm_gain[None],
        block_owner[0],
        block_base,
        frame_offset[0],
        team,
        streams,
        packs,
    )
    got = [sends[0]] + [swap(sends[e], "pack", packs, e) for e in range(1, packs)]
    return encoded[None], pool(got)[None]


def marks_turns(team, stream):
    dests = list(reversed(range(team)))
    return [dests[: team // 2], dests[team // 2 :]] if stream == 0 else [dests]


def far_turns(team, tm):
    return [other + d for other in range(team, tm, team) for d in reversed(range(team))]


def solution(mesh):
    tm = mesh.shape["tm"]
    team = tm // 2
    return jax.shard_map(
        functools.partial(local, team),
        mesh=mesh,
        in_specs=(
            P("pack", "tm", None),
            P("pack", "tm", None),
            P("pack", "tm", None),
            P(),
            P(),
            P("pack", "tm", None),
            P("pack", "tm"),
            P("pack", "tm", None),
        ),
        out_specs=(P("pack", "tm", None), P("pack", "tm", None)),
        check_vma=False,
    )
```
